32 devices in a mesh: gx: 8 (over y, x, core), gy: 4 (over z).
Axes of the slice: x: 2, y: 2, z: 4, core: 2. Of those that a mesh axis runs over, the one named last changes fastest.
Arguments:
- model_image: bfloat16 [16, 1024, 4096], P(None, 'gx', 'gy'), may hold values from -6 to 6
- tables: bfloat16 [8, 128, 1024], replicated, may hold values from -0.1875 to 0.1875
- observed: bfloat16 [1024, 16, 128], P(('gx', 'gy')), may hold values from -6 to 6
- aperture: int32 [1024, 4], P(('gx', 'gy')), may hold values from 0 to 31, all different within a row; in each aligned block of 32 rows (0 to 31, 32 to 63, ...) at most 8 rows name the same one
- traveltime: int32 [1024, 4, 16], P(('gx', 'gy')), may hold values from 0 to 15
- band_index: int32 [1024, 4, 16], P(('gx', 'gy')), may hold values from 0 to 7
- amplitude: bfloat16 [1024, 4, 128], P(('gx', 'gy')), may hold values from 0.019897461 to 0.19921875
Outputs:
- residual: float32 [1024, 16, 128], P(('gx', 'gy'))
- gradient: float32 [16, 1024, 4096], P(None, 'gx', 'gy')
The draws below stay inside these ranges and needn't reach their ends.
Inputs may be any that keep to these rules, and one draw needn't show every extreme that they name: `aperture`: each trace names 4 distinct tiles. Among the traces of one device no tile is named more than 8 times, a bound that some block reaches.
All inputs are finite; a program needn't handle non-finite values.
Results may differ from the reference program's by a relative error of at most 0.006.
Values may be sent and summed in bfloat16 or wider, within the bound.
No kernel may reach another device: no remote copies, remote signals or barrier semaphores. Data moves between devices by JAX's collectives and lax.ppermute only.
A program may use at most 64 MiB of HBM per device.

```python
import math
import jax
import jax.numpy as jnp
import numpy as np
from jax import lax

NZ = 16
BL = 128
NB = 16
NBAND = 8
K = 4
TR = 32
CX = 128
CY = 1024
CAP = 8
TRACES = 1024
NX = 1024
NY = 4096
N_GX = 8
N_GY = 4
DEVICES = 32


def touch_ends(result, key, low, largest):
    longest = result.shape.index(max(result.shape))
    spots = []
    for shift in (0, 1):
        where = [jax.random.randint(jax.random.fold_in(key, axis), (), 0, length) for axis, length in enumerate(result.shape)]
        where[longest] = (where[longest] + shift) % result.shape[longest]
        spots.append(tuple(where))
    return result.at[spots[0]].set(low).at[spots[1]].set(largest)


def levels(stream_key, dims, shards, smallest, top_value):
    def one(axis_at, parts):
        draws = jax.random.uniform(jax.random.fold_in(jax.random.fold_in(stream_key, 6), axis_at), (parts,), jnp.float32, smallest / len(shards), top_value / len(shards))
        return jnp.repeat(jnp.exp(draws), dims[axis_at] // parts).reshape((-1,) + (1,) * (len(dims) - axis_at - 1))

    gain = one(*shards[0])
    for cut in shards[1:]:
        gain = gain * one(*cut)
    return gain


def routed_block(own_key, own, number, rows, number_of, top, limit, slope):
    order = jax.random.permutation(own_key, number_of)
    packed, usual = load_shares(number_of, rows * top, limit, slope, True), load_shares(number_of, rows * top, limit, slope, False)
    places = jnp.arange(number_of)

    def named(sizes, rotation):
        used = int((sizes > 0).sum())
        fixed = max(1, used // 4)
        moved = fixed + (places - fixed + rotation * (used - fixed)) % max(1, number_of - fixed)
        return jnp.zeros((number_of,), jnp.int32).at[order[jnp.where(places < fixed, places, moved)]].set(jnp.asarray(sizes, jnp.int32))

    sizes = jnp.where(number % 4 == 0, named(packed, number // 4), named(usual, number - number // 4 - 1))
    mixed = jax.random.permutation(jax.random.fold_in(own, 3), number_of)
    source_of, taker = mixed[0:number_of // 2 * 2:2], mixed[1:number_of // 2 * 2:2]
    margin = jnp.minimum(sizes[source_of] - 1, limit - sizes[taker]) // 2
    margin = jnp.where((source_of == order[0]) | (taker == order[0]) | (sizes[taker] == 0), 0, jnp.maximum(margin, 0))
    moved = jax.random.randint(jax.random.fold_in(own, 4), (number_of // 2,), 0, 1 << 20) % (margin + 1)
    sizes = sizes.at[source_of].add(-moved).at[taker].add(moved)
    items = jnp.searchsorted(jnp.cumsum(sizes), jnp.arange(rows * top), side="right").astype(jnp.int32)
    listing = items.reshape(top, rows).T
    listing = listing[jax.random.permutation(jax.random.fold_in(own, 1), rows)]
    rotation = jax.random.randint(jax.random.fold_in(own, 2), (rows, 1), 0, top)
    return jnp.take_along_axis(listing, (jnp.arange(top)[None, :] + rotation) % top, axis=1)


def load_shares(count, total, bound, lean, full):
    loads = [(1 << 20) // math.isqrt(grade ** lean) + 1 for grade in range(1, count + 1)]
    largest = bound if full else min(bound, max(-(-total // count), total * loads[0] // sum(loads)))
    least = 1 if total - largest >= count - 1 else 0
    holding, spare = [largest] + [least] * (count - 1), total - largest - least * (count - 1)
    while spare > 0:
        candidates = [i for i in range(1, count) if holding[i] < largest] or [i for i in range(1, count) if holding[i] < bound]
        pool, remaining = sum([loads[i] for i in candidates]), spare
        for i in candidates:
            extra = min(bound - holding[i], max(1, remaining * loads[i] // pool), spare)
            holding[i] = holding[i] + extra
            spare = spare - extra
    return np.array(holding)


def noise(stream_key, shape, spread, limit, cuts=(), kind=jnp.bfloat16):
    values = jax.random.normal(stream_key, shape, jnp.float32) * spread
    if len(cuts) > 0:
        values = levels(stream_key, shape, cuts, -0.22, 0.18) * values
    return jnp.clip(values, min=-limit, max=limit).astype(kind)


def setup_inputs(seed: int = 0) -> dict:
    seeds = jax.random.split(jax.random.key(seed), 8)
    model_image = noise(seeds[0], (NZ, NX, NY), 1.0, 6.0, ((1, 8), (2, 4)))
    tables = noise(seeds[1], (NBAND, BL, CY), CY ** -0.5, 0.1875)
    observed = noise(seeds[2], (TRACES, NB, BL), 1.0, 6.0, ((0, 32),))
    aperture_keys = jax.random.split(jax.random.fold_in(seeds[3], 1), TRACES // TR)
    aperture_turns = jax.random.permutation(jax.random.fold_in(seeds[3], 3), TRACES // TR)
    aperture = jax.vmap(lambda own, number: routed_block(jax.random.fold_in(seeds[3], 2), own, number, TR, DEVICES, K, CAP, 2))(aperture_keys, aperture_turns).reshape((TRACES, K))
    traveltime = touch_ends(jax.random.randint(seeds[4], (TRACES, K, NZ), 0, NB), jax.random.fold_in(seeds[4], 1), 0, NB - 1).astype(jnp.int32)
    band_index = touch_ends(jax.random.randint(seeds[5], (TRACES, K, NZ), 0, NBAND), jax.random.fold_in(seeds[5], 1), 0, NBAND - 1).astype(jnp.int32)
    amplitude = jnp.clip(jnp.exp(math.log(0.19921875) - 2.3038113 * jax.random.uniform(seeds[6], (TRACES, K, CX), jnp.float32) ** levels(seeds[6], (TRACES, K, CX), ((0, 32),), -0.2, 0.2)), 0.019897461, 0.19921875).astype(jnp.bfloat16)
    return dict(model_image=model_image, tables=tables, observed=observed, aperture=aperture, traveltime=traveltime, band_index=band_index, amplitude=amplitude)


def reference(model_image, tables, observed, aperture, traveltime, band_index, amplitude):
    slot_count = DEVICES * CAP
    pair_count = TRACES * K
    destination = aperture.reshape(pair_count).astype(jnp.int32)
    order = jnp.argsort(destination, stable=True).astype(jnp.int32)
    counts = jnp.zeros((DEVICES,), jnp.int32).at[destination].add(1)
    starts = (jnp.cumsum(counts) - counts).astype(jnp.int32)
    amp_flat = amplitude.reshape(pair_count, CX)
    band_flat = band_index.reshape(pair_count, NZ)
    time_flat = traveltime.reshape(pair_count, NZ)
    tables_flat = tables.reshape(NBAND * BL, CY)
    band_picks = jnp.arange(NBAND, dtype=jnp.int32)
    image_tiles = model_image.reshape(NZ, N_GX, CX, N_GY, CY)

    def tile_lists(tile):
        offset = jnp.arange(slot_count, dtype=jnp.int32)
        live = offset < counts[tile]
        index = jnp.clip(starts[tile] + offset, 0, pair_count - 1).astype(jnp.int32)
        pair = order[index]
        amp_live = jnp.where(live[:, None], amp_flat[pair], jnp.zeros((), amp_flat.dtype))
        return pair, live, amp_live

    def tile_rows(tile):
        tile_x = tile // N_GY
        tile_y = tile % N_GY
        start = (jnp.int32(0), tile_x.astype(jnp.int32), jnp.int32(0), tile_y.astype(jnp.int32), jnp.int32(0))
        block = lax.dynamic_slice(image_tiles, start, (NZ, 1, CX, 1, CY)).reshape(NZ * CX, CY)
        rows = jnp.dot(block, tables_flat.T, preferred_element_type=jnp.float32)
        return rows.astype(jnp.bfloat16).reshape(NZ, CX, NBAND * BL)

    def model_tile(modeled, tile):
        pair, live, amp_live = tile_lists(tile)
        rows = tile_rows(tile)
        full = jnp.einsum("px,zxk->zpk", amp_live.astype(jnp.float32), rows.astype(jnp.float32))
        full = full.reshape(NZ, slot_count, NBAND, BL)
        pick = (band_flat[pair].T[:, :, None] == band_picks[None, None, :]).astype(jnp.float32)
        part = jnp.sum(full * pick[..., None], axis=2).astype(jnp.bfloat16)
        trace = (pair // K).astype(jnp.int32)
        trace_idx = jnp.broadcast_to(trace[None, :], (NZ, slot_count))
        block_idx = time_flat[pair].T
        values = part.astype(jnp.float32) * live.astype(jnp.float32)[None, :, None]
        return modeled.at[trace_idx, block_idx].add(values), None

    modeled, _ = lax.scan(model_tile, jnp.zeros((TRACES, NB, BL), jnp.float32), jnp.arange(DEVICES, dtype=jnp.int32))
    residual = modeled - observed.astype(jnp.float32)
    residual_bf = residual.astype(jnp.bfloat16)

    def image_tile(tile):
        pair, live, amp_live = tile_lists(tile)
        trace = (pair // K).astype(jnp.int32)
        trace_idx = jnp.broadcast_to(trace[None, :], (NZ, slot_count))
        blocks = residual_bf[trace_idx, time_flat[pair].T]
        pick = (band_flat[pair].T[:, :, None] == band_picks[None, None, :]).astype(jnp.bfloat16)
        masked = (pick[..., None] * blocks[:, :, None, :]).reshape(NZ, slot_count, NBAND * BL)
        stacks = jnp.einsum("px,zpk->zxk", amp_live.astype(jnp.float32), masked.astype(jnp.float32)).astype(jnp.bfloat16)
        grad = jnp.dot(stacks.reshape(NZ * CX, NBAND * BL), tables_flat, preferred_element_type=jnp.float32)
        return grad.reshape(NZ, CX, CY)

    grads = lax.map(image_tile, jnp.arange(DEVICES, dtype=jnp.int32))
    gradient = grads.reshape(N_GX, N_GY, NZ, CX, CY).transpose(2, 0, 3, 1, 4).reshape(NZ, NX, NY)
    return residual, gradient
```

```python
import functools

import jax
import jax.numpy as jnp
from jax import lax
from jax.experimental import pallas as pl
from jax.experimental.pallas import tpu as pltpu
from jax.sharding import PartitionSpec as P

BF = jnp.bfloat16
F32 = jnp.float32
VMEM = pl.BlockSpec(memory_space=pltpu.VMEM)
SMEM = pl.BlockSpec(memory_space=pltpu.SMEM)


def dot(a, b, dims=((1,), (0,))):
    return lax.dot_general(a, b, (dims, ((), ())), preferred_element_type=F32)


def iota(shape, axis):
    return lax.broadcasted_iota(jnp.int32, shape, axis)


def prep_kernel(devices, capacity, ap_ref, tt_ref, bi_ref, am_ref, msg_ref, pos_ref):
    tiles, traces = ap_ref.shape
    slots = devices * capacity
    width = am_ref.shape[2]
    depth = tt_ref.shape[1]
    before = (iota((traces, traces), 0) < iota((traces, traces), 1)).astype(BF)
    base = jnp.zeros((devices, 1), F32)
    amp = jnp.zeros((slots, width), F32)
    marks = jnp.zeros((slots, width), F32)
    for k in range(tiles):
        dest = ap_ref[k : k + 1, :]
        hit = iota((devices, traces), 0) == dest
        hits = hit.astype(F32)
        rank = jnp.sum(hits * (base + dot(hits.astype(BF), before)), axis=0, keepdims=True)
        base = base + jnp.sum(hits, axis=1, keepdims=True)
        pos = dest * capacity + rank.astype(jnp.int32)
        pos_ref[k : k + 1, :] = pos
        place = (iota((slots, traces), 0) == pos).astype(F32).astype(BF)
        amp = amp + dot(place, am_ref[:, k, :])
        levels = jnp.concatenate(
            [
                bi_ref[k].astype(F32),
                tt_ref[k].astype(F32),
                jnp.zeros((width - 2 * depth, traces), F32),
            ],
            axis=0,
        ).astype(BF)
        marks = marks + dot(place, levels, ((1,), (1,)))
    msg_ref[:, :width] = amp.astype(BF)
    msg_ref[:, width:] = marks.astype(BF)


def spread(marks, lane):
    width = marks.shape[1]
    return dot(marks, (iota((width, width), 0) == lane).astype(F32).astype(BF))


def demig_kernel(bands, blocks, msg_ref, rows_ref, out_ref, part_ref, time_ref):
    z = pl.program_id(0)
    depth, slots, block_len = part_ref.shape
    width = rows_ref.shape[1]
    amp = msg_ref[:, :width]
    marks = msg_ref[:, width:]
    band = spread(marks, z)
    time_ref[z] = spread(marks, z + depth).astype(BF)
    zero = jnp.zeros_like(amp)
    weights = jnp.concatenate([jnp.where(band == b, amp, zero) for b in range(bands)], axis=1)
    rows = jnp.concatenate(
        [rows_ref[0, :, b * block_len : (b + 1) * block_len] for b in range(bands)], axis=0
    )
    part_ref[z] = dot(weights, rows).astype(BF)

    @pl.when(z == depth - 1)
    def _():
        group = 256 // depth

        def one(g, carry):
            at = pl.ds(pl.multiple_of(g * group, group), group)
            pick = picker(time_ref[:, at, :], blocks)
            part = part_ref[:, at, :].reshape(depth * group, block_len)
            total = dot(pick, part, ((0,), (0,)))
            out_ref[at] = total.astype(BF).reshape(group, blocks, block_len)
            return carry

        lax.fori_loop(0, slots // group, one, 0)


def picker(times, blocks):
    depth, group, lanes = times.shape
    code = times.astype(F32).reshape(depth * group, lanes)
    own = (iota((depth * group, lanes), 0) % group * blocks).astype(F32)
    code = code + own
    at = iota((depth * group, lanes), 1).astype(F32)
    return jnp.concatenate(
        [(code == at + float(i)).astype(F32).astype(BF) for i in range(0, group * blocks, lanes)],
        axis=1,
    )


def residual_kernel(capacity, pos_ref, recv_ref, obs_ref, res_ref, send_ref):
    tiles, traces = pos_ref.shape
    send_ref[...] = jnp.zeros_like(send_ref)

    def one(t, carry):
        total = recv_ref[pos_ref[0, t]].astype(F32)
        for k in range(1, tiles):
            total = total + recv_ref[pos_ref[k, t]].astype(F32)
        total = total - obs_ref[t].astype(F32)
        res_ref[t] = total
        low = total.astype(BF)
        for k in range(tiles):
            send_ref[pos_ref[k, t]] = low
        return carry

    lax.fori_loop(0, traces, one, 0)


def image_kernel(bands, levels, msg_ref, blk_ref, tab_ref, out_ref, pick_ref, time_ref, amp_ref, stack_ref):
    step = pl.program_id(0)
    depth, slots, block_len = pick_ref.shape
    blocks = blk_ref.shape[1]
    width = out_ref.shape[1]
    marks = msg_ref[:, width:]

    @pl.when(step == 0)
    def _():
        amp_ref[...] = msg_ref[:, :width].astype(F32).T.astype(BF)
        for z in range(depth):
            time_ref[z] = spread(marks, z + depth).astype(BF)
        group = 256 // depth

        def one(g, carry):
            at = pl.ds(pl.multiple_of(g * group, group), group)
            pick = picker(time_ref[:, at, :], blocks)
            block = blk_ref[at].reshape(group * blocks, block_len)
            pick_ref[:, at, :] = dot(pick, block).astype(BF).reshape(depth, group, block_len)
            return carry

        lax.fori_loop(0, slots // group, one, 0)

    for i in range(levels):
        z = step * levels + i
        band = spread(marks, z)
        picked = pick_ref[z]
        zero = jnp.zeros_like(picked)
        masked = jnp.concatenate([jnp.where(band == b, picked, zero) for b in range(bands)], axis=1)
        stack_ref[i * width : (i + 1) * width, :] = dot(amp_ref[...], masked).astype(BF)
    image = dot(stack_ref[...], tab_ref[...])
    out_ref[...] = image.reshape(levels, width, image.shape[1])


def shards(model_image, tables, observed, aperture, traveltime, band_index, amplitude):
    devices = lax.axis_size("gx") * lax.axis_size("gy")
    depth, width_x, width_y = model_image.shape
    bands, block_len, _ = tables.shape
    traces, tile_count = aperture.shape
    blocks = observed.shape[1]
    capacity = max(2, 2 * traces * tile_count // devices)
    slots = devices * capacity
    tables_flat = tables.reshape(bands * block_len, width_y)

    message, position = pl.pallas_call(
        functools.partial(prep_kernel, devices, capacity),
        out_shape=(
            jax.ShapeDtypeStruct((slots, 2 * width_x), BF),
            jax.ShapeDtypeStruct((tile_count, traces), jnp.int32),
        ),
        in_specs=[VMEM] * 4,
        out_specs=(VMEM, VMEM),
        name="prep",
    )(
        aperture.T,
        traveltime.transpose(1, 2, 0),
        band_index.transpose(1, 2, 0),
        amplitude,
    )
    got = lax.all_to_all(message, ("gx", "gy"), split_axis=0, concat_axis=0, tiled=True)
    rows = lax.dot_general(
        model_image.reshape(depth * width_x, width_y),
        tables_flat,
        (((1,), (1,)), ((), ())),
        preferred_element_type=F32,
    )
    rows = rows.astype(BF).reshape(depth, width_x, bands * block_len)

    modeled = pl.pallas_call(
        functools.partial(demig_kernel, bands, blocks),
        grid=(depth,),
        out_shape=jax.ShapeDtypeStruct((slots, blocks, block_len), BF),
        in_specs=[
            pl.BlockSpec((slots, 2 * width_x), lambda z: (0, 0)),
            pl.BlockSpec((1, width_x, bands * block_len), lambda z: (z, 0, 0)),
        ],
        out_specs=pl.BlockSpec((slots, blocks, block_len), lambda z: (0, 0, 0)),
        scratch_shapes=[
            pltpu.VMEM((depth, slots, block_len), BF),
            pltpu.VMEM((depth, slots, width_x), BF),
        ],
        compiler_params=pltpu.CompilerParams(dimension_semantics=("arbitrary",)),
        name="demig",
    )(got, rows)
    returned = lax.all_to_all(modeled, ("gx", "gy"), split_axis=0, concat_axis=0, tiled=True)
    residual, outgoing = pl.pallas_call(
        functools.partial(residual_kernel, capacity),
        out_shape=(
            jax.ShapeDtypeStruct((traces, blocks, block_len), F32),
            jax.ShapeDtypeStruct((slots, blocks, block_len), BF),
        ),
        in_specs=[SMEM, VMEM, VMEM],
        out_specs=(VMEM, VMEM),
        name="resid",
    )(position, returned, observed)
    incoming = lax.all_to_all(outgoing, ("gx", "gy"), split_axis=0, concat_axis=0, tiled=True)
    levels = 4
    gradient = pl.pallas_call(
        functools.partial(image_kernel, bands, levels),
        grid=(depth // levels,),
        out_shape=jax.ShapeDtypeStruct((depth, width_x, width_y), F32),
        in_specs=[
            pl.BlockSpec((slots, 2 * width_x), lambda z: (0, 0)),
            pl.BlockSpec((slots, blocks, block_len), lambda z: (0, 0, 0)),
            pl.BlockSpec((bands * block_len, width_y), lambda z: (0, 0)),
        ],
        out_specs=pl.BlockSpec((levels, width_x, width_y), lambda z: (z, 0, 0)),
        scratch_shapes=[
            pltpu.VMEM((depth, slots, block_len), BF),
            pltpu.VMEM((depth, slots, width_x), BF),
            pltpu.VMEM((width_x, slots), BF),
            pltpu.VMEM((levels * width_x, bands * block_len), BF),
        ],
        compiler_params=pltpu.CompilerParams(dimension_semantics=("arbitrary",)),
        name="image",
    )(got, incoming, tables_flat)
    return residual, gradient


def solution(mesh):
    both = ("gx", "gy")
    placed = (
        P(None, "gx", "gy"),
        P(),
        P(both, None, None),
        P(both, None),
        P(both, None, None),
        P(both, None, None),
        P(both, None, None),
    )
    return jax.shard_map(
        shards,
        mesh=mesh,
        in_specs=placed,
        out_specs=(P(both, None, None), P(None, "gx", "gy")),
        check_vma=False,
    )
```

```python
import functools

import jax
import jax.numpy as jnp
from jax import lax
from jax.experimental import pallas as pl
from jax.experimental.pallas import tpu as pltpu
from jax.sharding import PartitionSpec as P

BF = jnp.bfloat16
F32 = jnp.float32
VMEM = pl.BlockSpec(memory_space=pltpu.VMEM)
SMEM = pl.BlockSpec(memory_space=pltpu.SMEM)


def dot(a, b, dims=((1,), (0,))):
    return lax.dot_general(a, b, (dims, ((), ())), preferred_element_type=F32)


def iota(shape, axis):
    return lax.broadcasted_iota(jnp.int32, shape, axis)


def prep_kernel(devices, capacity, ap_ref, tt_ref, bi_ref, am_ref, msg_ref, pos_ref):
    tiles, traces = ap_ref.shape
    slots = devices * capacity
    width = am_ref.shape[2]
    depth = tt_ref.shape[1]
    before = (iota((traces, traces), 0) < iota((traces, traces), 1)).astype(BF)
    base = jnp.zeros((devices, 1), F32)
    amp = jnp.zeros((slots, width), F32)
    marks = jnp.zeros((slots, width), F32)
    for k in range(tiles):
        dest = ap_ref[k : k + 1, :]
        hit = iota((devices, traces), 0) == dest
        hits = hit.astype(F32)
        rank = jnp.sum(hits * (base + dot(hits.astype(BF), before)), axis=0, keepdims=True)
        base = base + jnp.sum(hits, axis=1, keepdims=True)
        pos = dest * capacity + rank.astype(jnp.int32)
        pos_ref[k : k + 1, :] = pos
        place = (iota((slots, traces), 0) == pos).astype(F32).astype(BF)
        amp = amp + dot(place, am_ref[:, k, :])
        levels = jnp.concatenate(
            [
                bi_ref[k].astype(F32),
                tt_ref[k].astype(F32),
                jnp.zeros((width - 2 * depth, traces), F32),
            ],
            axis=0,
        ).astype(BF)
        marks = marks + dot(place, levels, ((1,), (1,)))
    msg_ref[:, :width] = amp.astype(BF)
    msg_ref[:, width:] = marks.astype(BF)


def spread(marks, first, second):
    width = marks.shape[1]
    lane = iota((width, 2 * width), 1)
    want = jnp.where(lane < width, first, second)
    return dot(marks, (iota((width, 2 * width), 0) == want).astype(F32).astype(BF)).astype(BF)


def by_band(band, values, bands):
    zero = jnp.zeros_like(values)
    return jnp.concatenate([jnp.where(band == BF(b), values, zero) for b in range(bands)], axis=1)


def demig_kernel(bands, blocks, levels, msg_ref, rows_ref, out_ref, part_ref, time_ref):
    step = pl.program_id(0)
    depth, slots, block_len = part_ref.shape
    width = rows_ref.shape[1]
    amp = msg_ref[:, :width]
    marks = msg_ref[:, width:]
    for i in range(levels):
        z = step * levels + i
        both = spread(marks, z, z + depth)
        time_ref[z] = both[:, width:]
        rows = jnp.concatenate(
            [rows_ref[i, :, b * block_len : (b + 1) * block_len] for b in range(bands)], axis=0
        )
        part_ref[z] = dot(by_band(both[:, :width], amp, bands), rows).astype(BF)

    @pl.when(step == pl.num_programs(0) - 1)
    def _():
        group = 256 // depth

        def one(g, carry):
            at = pl.ds(pl.multiple_of(g * group, group), group)
            pick = picker(time_ref[:, at, :], blocks)
            part = part_ref[:, at, :].reshape(depth * group, block_len)
            total = dot(pick, part, ((0,), (0,)))
            out_ref[at] = total.astype(BF).reshape(group, blocks, block_len)
            return carry

        lax.fori_loop(0, slots // group, one, 0, unroll=4)


def picker(times, blocks):
    depth, group, lanes = times.shape
    code = times.astype(F32).reshape(depth * group, lanes)
    own = (iota((depth * group, lanes), 0) % group * blocks).astype(F32)
    code = code + own
    at = iota((depth * group, lanes), 1).astype(F32)
    return jnp.concatenate(
        [(code == at + float(i)).astype(F32).astype(BF) for i in range(0, group * blocks, lanes)],
        axis=1,
    )


def residual_kernel(capacity, pos_ref, recv_ref, obs_ref, res_ref, send_ref):
    tiles, traces = pos_ref.shape
    send_ref[...] = jnp.zeros_like(send_ref)

    def one(t, carry):
        total = recv_ref[pos_ref[0, t]].astype(F32)
        for k in range(1, tiles):
            total = total + recv_ref[pos_ref[k, t]].astype(F32)
        total = total - obs_ref[t].astype(F32)
        res_ref[t] = total
        low = total.astype(BF)
        for k in range(tiles):
            send_ref[pos_ref[k, t]] = low
        return carry

    lax.fori_loop(0, traces, one, 0)


def image_kernel(bands, levels, msg_ref, blk_ref, tab_ref, out_ref, pick_ref, time_ref, amp_ref, stack_ref):
    step = pl.program_id(0)
    depth, slots, block_len = pick_ref.shape
    blocks = blk_ref.shape[1]
    width = out_ref.shape[1]
    marks = msg_ref[:, width:]

    @pl.when(step == 0)
    def _():
        amp_ref[...] = msg_ref[:, :width].astype(F32).T.astype(BF)
        for z in range(0, depth, 2):
            both = spread(marks, z + depth, z + 1 + depth)
            time_ref[z] = both[:, :width]
            time_ref[z + 1] = both[:, width:]
        group = 256 // depth

        def one(g, carry):
            at = pl.ds(pl.multiple_of(g * group, group), group)
            pick = picker(time_ref[:, at, :], blocks)
            block = blk_ref[at].reshape(group * blocks, block_len)
            pick_ref[:, at, :] = dot(pick, block).astype(BF).reshape(depth, group, block_len)
            return carry

        lax.fori_loop(0, slots // group, one, 0, unroll=4)

    for i in range(0, levels, 2):
        z = step * levels + i
        both = spread(marks, z, z + 1)
        for j in range(2):
            masked = by_band(both[:, j * width : (j + 1) * width], pick_ref[z + j], bands)
            stack = dot(amp_ref[...], masked)
            stack_ref[(i + j) * width : (i + j + 1) * width, :] = stack.astype(BF)
    image = dot(stack_ref[...], tab_ref[...])
    out_ref[...] = image.reshape(levels, width, image.shape[1])


def shards(model_image, tables, observed, aperture, traveltime, band_index, amplitude):
    devices = lax.axis_size("gx") * lax.axis_size("gy")
    depth, width_x, width_y = model_image.shape
    bands, block_len, _ = tables.shape
    traces, tile_count = aperture.shape
    blocks = observed.shape[1]
    capacity = max(2, 2 * traces * tile_count // devices)
    slots = devices * capacity
    levels = 4
    tables_flat = tables.reshape(bands * block_len, width_y)

    message, position = pl.pallas_call(
        functools.partial(prep_kernel, devices, capacity),
        out_shape=(
            jax.ShapeDtypeStruct((slots, 2 * width_x), BF),
            jax.ShapeDtypeStruct((tile_count, traces), jnp.int32),
        ),
        in_specs=[VMEM] * 4,
        out_specs=(VMEM, VMEM),
        name="prep",
    )(
        aperture.T,
        traveltime.transpose(1, 2, 0),
        band_index.transpose(1, 2, 0),
        amplitude,
    )
    got = lax.all_to_all(message, ("gx", "gy"), split_axis=0, concat_axis=0, tiled=True)
    rows = lax.dot_general(
        model_image.reshape(depth * width_x, width_y),
        tables_flat,
        (((1,), (1,)), ((), ())),
        preferred_element_type=F32,
    )
    rows = rows.astype(BF).reshape(depth, width_x, bands * block_len)

    modeled = pl.pallas_call(
        functools.partial(demig_kernel, bands, blocks, levels),
        grid=(depth // levels,),
        out_shape=jax.ShapeDtypeStruct((slots, blocks, block_len), BF),
        in_specs=[
            pl.BlockSpec((slots, 2 * width_x), lambda z: (0, 0)),
            pl.BlockSpec((levels, width_x, bands * block_len), lambda z: (z, 0, 0)),
        ],
        out_specs=pl.BlockSpec((slots, blocks, block_len), lambda z: (0, 0, 0)),
        scratch_shapes=[
            pltpu.VMEM((depth, slots, block_len), BF),
            pltpu.VMEM((depth, slots, width_x), BF),
        ],
        compiler_params=pltpu.CompilerParams(dimension_semantics=("arbitrary",)),
        name="demig",
    )(got, rows)
    returned = lax.all_to_all(modeled, ("gx", "gy"), split_axis=0, concat_axis=0, tiled=True)
    residual, outgoing = pl.pallas_call(
        functools.partial(residual_kernel, capacity),
        out_shape=(
            jax.ShapeDtypeStruct((traces, blocks, block_len), F32),
            jax.ShapeDtypeStruct((slots, blocks, block_len), BF),
        ),
        in_specs=[SMEM, VMEM, VMEM],
        out_specs=(VMEM, VMEM),
        name="resid",
    )(position, returned, observed)
    incoming = lax.all_to_all(outgoing, ("gx", "gy"), split_axis=0, concat_axis=0, tiled=True)
    gradient = pl.pallas_call(
        functools.partial(image_kernel, bands, levels),
        grid=(depth // levels,),
        out_shape=jax.ShapeDtypeStruct((depth, width_x, width_y), F32),
        in_specs=[
            pl.BlockSpec((slots, 2 * width_x), lambda z: (0, 0)),
            pl.BlockSpec((slots, blocks, block_len), lambda z: (0, 0, 0)),
            pl.BlockSpec((bands * block_len, width_y), lambda z: (0, 0)),
        ],
        out_specs=pl.BlockSpec((levels, width_x, width_y), lambda z: (z, 0, 0)),
        scratch_shapes=[
            pltpu.VMEM((depth, slots, block_len), BF),
            pltpu.VMEM((depth, slots, width_x), BF),
            pltpu.VMEM((width_x, slots), BF),
            pltpu.VMEM((levels * width_x, bands * block_len), BF),
        ],
        compiler_params=pltpu.CompilerParams(dimension_semantics=("arbitrary",)),
        name="image",
    )(got, incoming, tables_flat)
    return residual, gradient


def solution(mesh):
    both = ("gx", "gy")
    placed = (
        P(None, "gx", "gy"),
        P(),
        P(both, None, None),
        P(both, None),
        P(both, None, None),
        P(both, None, None),
        P(both, None, None),
    )
    return jax.shard_map(
        shards,
        mesh=mesh,
        in_specs=placed,
        out_specs=(P(both, None, None), P(None, "gx", "gy")),
        check_vma=False,
    )
```

```python
import functools

import jax
import jax.numpy as jnp
from jax import lax
from jax.experimental import pallas as pl
from jax.experimental.pallas import tpu as pltpu
from jax.sharding import PartitionSpec as P

BF = jnp.bfloat16
F32 = jnp.float32
GRANT = pltpu.CompilerParams(vmem_limit_bytes=20 * 1024 * 1024)
VMEM = pl.BlockSpec(memory_space=pltpu.VMEM)
SMEM = pl.BlockSpec(memory_space=pltpu.SMEM)


def dot(a, b, dims=((1,), (0,))):
    return lax.dot_general(a, b, (dims, ((), ())), preferred_element_type=F32)


def iota(shape, axis):
    return lax.broadcasted_iota(jnp.int32, shape, axis)


def prep_kernel(devices, capacity, ap_ref, tt_ref, bi_ref, am_ref, msg_ref, pos_ref):
    tiles, traces = ap_ref.shape
    slots = devices * capacity
    width = am_ref.shape[2]
    depth = tt_ref.shape[1]
    before = (iota((traces, traces), 0) < iota((traces, traces), 1)).astype(BF)
    base = jnp.zeros((devices, 1), F32)
    amp = jnp.zeros((slots, width), F32)
    marks = jnp.zeros((slots, width), F32)
    for k in range(tiles):
        dest = ap_ref[k : k + 1, :]
        hit = iota((devices, traces), 0) == dest
        hits = hit.astype(F32)
        rank = jnp.sum(hits * (base + dot(hits.astype(BF), before)), axis=0, keepdims=True)
        base = base + jnp.sum(hits, axis=1, keepdims=True)
        pos = dest * capacity + rank.astype(jnp.int32)
        pos_ref[k : k + 1, :] = pos
        place = (iota((slots, traces), 0) == pos).astype(F32).astype(BF)
        amp = amp + dot(place, am_ref[:, k, :])
        levels = jnp.concatenate(
            [
                bi_ref[k].astype(F32),
                tt_ref[k].astype(F32),
                jnp.zeros((width - 2 * depth, traces), F32),
            ],
            axis=0,
        ).astype(BF)
        marks = marks + dot(place, levels, ((1,), (1,)))
    msg_ref[:, :width] = amp.astype(BF)
    msg_ref[:, width:] = marks.astype(BF)


def rows_kernel(image_ref, tab_ref, out_ref):
    levels, width, cells = image_ref.shape
    rows = dot(image_ref[...].reshape(levels * width, cells), tab_ref[...], ((1,), (1,)))
    out_ref[...] = rows.astype(BF).reshape(out_ref.shape)


def spread(marks, first, second):
    width = marks.shape[1]
    lane = iota((width, 2 * width), 1)
    want = jnp.where(lane < width, first, second)
    return dot(marks, (iota((width, 2 * width), 0) == want).astype(F32).astype(BF)).astype(BF)


def by_band(band, values, bands):
    zero = jnp.zeros_like(values)
    return jnp.concatenate([jnp.where(band == BF(b), values, zero) for b in range(bands)], axis=1)


def demig_kernel(bands, blocks, levels, msg_ref, rows_ref, out_ref, part_ref, time_ref):
    step = pl.program_id(0)
    depth, slots, block_len = part_ref.shape
    width = rows_ref.shape[1]
    amp = msg_ref[:, :width]
    marks = msg_ref[:, width:]
    for i in range(levels):
        z = step * levels + i
        both = spread(marks, z, z + depth)
        time_ref[z] = both[:, width:]
        rows = jnp.concatenate(
            [rows_ref[i, :, b * block_len : (b + 1) * block_len] for b in range(bands)], axis=0
        )
        part_ref[z] = dot(by_band(both[:, :width], amp, bands), rows).astype(BF)

    @pl.when(step == pl.num_programs(0) - 1)
    def _():
        group = 256 // depth

        def one(g, carry):
            at = pl.ds(pl.multiple_of(g * group, group), group)
            pick = picker(time_ref[:, at, :], blocks)
            part = part_ref[:, at, :].reshape(depth * group, block_len)
            total = dot(pick, part, ((0,), (0,)))
            out_ref[at] = total.astype(BF).reshape(group, blocks, block_len)
            return carry

        lax.fori_loop(0, slots // group, one, 0, unroll=4)


def picker(times, blocks):
    depth, group, lanes = times.shape
    own = (iota((group, lanes), 0) * blocks).astype(F32).astype(BF)
    code = (times + own[None]).reshape(depth * group, lanes)
    at = iota(code.shape, 1).astype(F32).astype(BF)
    one, zero = jnp.ones_like(code), jnp.zeros_like(code)
    return jnp.concatenate(
        [jnp.where(code == at + BF(i), one, zero) for i in range(0, group * blocks, lanes)], axis=1
    )


def residual_kernel(capacity, pos_ref, recv_ref, obs_ref, res_ref, send_ref):
    tiles, traces = pos_ref.shape
    send_ref[...] = jnp.zeros_like(send_ref)

    def one(t, carry):
        at = [pos_ref[k, t] for k in range(tiles)]
        total = recv_ref[at[0]].astype(F32)
        for k in range(1, tiles):
            total = total + recv_ref[at[k]].astype(F32)
        total = total - obs_ref[t].astype(F32)
        res_ref[t] = total
        low = total.astype(BF)
        for k in range(tiles):
            send_ref[at[k]] = low
        return carry

    lax.fori_loop(0, traces, one, 0, unroll=4)


def image_kernel(bands, levels, msg_ref, blk_ref, tab_ref, out_ref, pick_ref, time_ref, amp_ref, stack_ref):
    step = pl.program_id(0)
    depth, slots, block_len = pick_ref.shape
    blocks = blk_ref.shape[1]
    width = out_ref.shape[1]
    marks = msg_ref[:, width:]

    @pl.when(step == 0)
    def _():
        amp_ref[...] = msg_ref[:, :width].astype(F32).T.astype(BF)
        for z in range(0, depth, 2):
            both = spread(marks, z + depth, z + 1 + depth)
            time_ref[z] = both[:, :width]
            time_ref[z + 1] = both[:, width:]
        group = 256 // depth

        def one(g, carry):
            at = pl.ds(pl.multiple_of(g * group, group), group)
            pick = picker(time_ref[:, at, :], blocks)
            block = blk_ref[at].reshape(group * blocks, block_len)
            pick_ref[:, at, :] = dot(pick, block).astype(BF).reshape(depth, group, block_len)
            return carry

        lax.fori_loop(0, slots // group, one, 0, unroll=4)

    for i in range(0, levels, 2):
        z = step * levels + i
        both = spread(marks, z, z + 1)
        for j in range(2):
            masked = by_band(both[:, j * width : (j + 1) * width], pick_ref[z + j], bands)
            stack = dot(amp_ref[...], masked)
            stack_ref[(i + j) * width : (i + j + 1) * width, :] = stack.astype(BF)
    image = dot(stack_ref[...], tab_ref[...])
    out_ref[...] = image.reshape(levels, width, image.shape[1])


def shards(model_image, tables, observed, aperture, traveltime, band_index, amplitude):
    devices = lax.axis_size("gx") * lax.axis_size("gy")
    depth, width_x, width_y = model_image.shape
    bands, block_len, _ = tables.shape
    traces, tile_count = aperture.shape
    blocks = observed.shape[1]
    capacity = max(2, 2 * traces * tile_count // devices)
    slots = devices * capacity
    levels = 4
    tables_flat = tables.reshape(bands * block_len, width_y)

    message, position = pl.pallas_call(
        functools.partial(prep_kernel, devices, capacity),
        out_shape=(
            jax.ShapeDtypeStruct((slots, 2 * width_x), BF),
            jax.ShapeDtypeStruct((tile_count, traces), jnp.int32),
        ),
        in_specs=[VMEM] * 4,
        out_specs=(VMEM, VMEM),
        name="prep",
    )(
        aperture.T,
        traveltime.transpose(1, 2, 0),
        band_index.transpose(1, 2, 0),
        amplitude,
    )
    got = lax.all_to_all(message, ("gx", "gy"), split_axis=0, concat_axis=0, tiled=True)
    rows = pl.pallas_call(
        rows_kernel,
        grid=(depth // levels,),
        out_shape=jax.ShapeDtypeStruct((depth, width_x, bands * block_len), BF),
        in_specs=[
            pl.BlockSpec((levels, width_x, width_y), lambda z: (z, 0, 0)),
            pl.BlockSpec((bands * block_len, width_y), lambda z: (0, 0)),
        ],
        out_specs=pl.BlockSpec((levels, width_x, bands * block_len), lambda z: (z, 0, 0)),
        cost_estimate=pl.CostEstimate(
            flops=2 * depth * width_x * width_y * bands * block_len,
            bytes_accessed=4 * depth * width_x * width_y,
            transcendentals=0,
        ),
        name="rows",
    )(model_image, tables_flat)
    rows = pltpu.with_memory_space_constraint(rows, pltpu.HBM)
    modeled = pl.pallas_call(
        functools.partial(demig_kernel, bands, blocks, levels),
        grid=(depth // levels,),
        out_shape=jax.ShapeDtypeStruct((slots, blocks, block_len), BF),
        in_specs=[
            pl.BlockSpec((slots, 2 * width_x), lambda z: (0, 0)),
            pl.BlockSpec((levels, width_x, bands * block_len), lambda z: (z, 0, 0)),
        ],
        out_specs=pl.BlockSpec((slots, blocks, block_len), lambda z: (0, 0, 0)),
        scratch_shapes=[
            pltpu.VMEM((depth, slots, block_len), BF),
            pltpu.VMEM((depth, slots, width_x), BF),
        ],
        compiler_params=GRANT,
        name="demig",
    )(got, rows)
    returned = lax.all_to_all(modeled, ("gx", "gy"), split_axis=0, concat_axis=0, tiled=True)
    residual, outgoing = pl.pallas_call(
        functools.partial(residual_kernel, capacity),
        out_shape=(
            jax.ShapeDtypeStruct((traces, blocks, block_len), F32),
            jax.ShapeDtypeStruct((slots, blocks, block_len), BF),
        ),
        in_specs=[SMEM, VMEM, VMEM],
        out_specs=(VMEM, VMEM),
        compiler_params=GRANT,
        name="resid",
    )(position, returned, observed)
    incoming = lax.all_to_all(outgoing, ("gx", "gy"), split_axis=0, concat_axis=0, tiled=True)
    gradient = pl.pallas_call(
        functools.partial(image_kernel, bands, levels),
        grid=(depth // levels,),
        out_shape=jax.ShapeDtypeStruct((depth, width_x, width_y), F32),
        in_specs=[
            pl.BlockSpec((slots, 2 * width_x), lambda z: (0, 0)),
            pl.BlockSpec((slots, blocks, block_len), lambda z: (0, 0, 0)),
            pl.BlockSpec((bands * block_len, width_y), lambda z: (0, 0)),
        ],
        out_specs=pl.BlockSpec((levels, width_x, width_y), lambda z: (z, 0, 0)),
        scratch_shapes=[
            pltpu.VMEM((depth, slots, block_len), BF),
            pltpu.VMEM((depth, slots, width_x), BF),
            pltpu.VMEM((width_x, slots), BF),
            pltpu.VMEM((levels * width_x, bands * block_len), BF),
        ],
        compiler_params=GRANT,
        name="image",
    )(got, incoming, tables_flat)
    return residual, gradient


def solution(mesh):
    both = ("gx", "gy")
    placed = (
        P(None, "gx", "gy"),
        P(),
        P(both, None, None),
        P(both, None),
        P(both, None, None),
        P(both, None, None),
        P(both, None, None),
    )
    return jax.shard_map(
        shards,
        mesh=mesh,
        in_specs=placed,
        out_specs=(P(both, None, None), P(None, "gx", "gy")),
        check_vma=False,
    )
```

```python
import functools

import jax
import jax.numpy as jnp
from jax import lax
from jax.experimental import pallas as pl
from jax.experimental.pallas import tpu as pltpu
from jax.sharding import PartitionSpec as P

BF = jnp.bfloat16
F32 = jnp.float32
GRANT = pltpu.CompilerParams(vmem_limit_bytes=20 * 1024 * 1024)
VMEM = pl.BlockSpec(memory_space=pltpu.VMEM)


def dot(a, b, dims=((1,), (0,))):
    return lax.dot_general(a, b, (dims, ((), ())), preferred_element_type=F32)


def iota(shape, axis):
    return lax.broadcasted_iota(jnp.int32, shape, axis)


def prep_kernel(devices, capacity, ap_ref, bi_ref, am_ref, msg_ref, place_ref):
    tiles, traces = ap_ref.shape
    slots = devices * capacity
    width = am_ref.shape[2]
    depth = bi_ref.shape[1]
    before = (iota((traces, traces), 0) < iota((traces, traces), 1)).astype(BF)
    base = jnp.zeros((devices, 1), F32)
    amp = jnp.zeros((slots, width), F32)
    marks = jnp.zeros((slots, width), F32)
    for k in range(tiles):
        dest = ap_ref[k : k + 1, :]
        hit = iota((devices, traces), 0) == dest
        hits = hit.astype(F32)
        rank = jnp.sum(hits * (base + dot(hits.astype(BF), before)), axis=0, keepdims=True)
        base = base + jnp.sum(hits, axis=1, keepdims=True)
        pos = dest * capacity + rank.astype(jnp.int32)
        place = (iota((slots, traces), 0) == pos).astype(F32).astype(BF)
        place_ref[:, k * traces : (k + 1) * traces] = place
        amp = amp + dot(place, am_ref[:, k, :])
        levels = jnp.concatenate(
            [bi_ref[k].astype(F32), jnp.zeros((width - depth, traces), F32)], axis=0
        ).astype(BF)
        marks = marks + dot(place, levels, ((1,), (1,)))
    msg_ref[:, :width] = amp.astype(BF)
    msg_ref[:, width:] = marks.astype(BF)


def codes_kernel(blocks, place_ref, tt_ref, take_ref, pick_ref, drop_ref):
    tiles, depth, traces = tt_ref.shape
    group = 256 // blocks
    take_ref[...] = place_ref[...].astype(F32).T.astype(BF)
    size = depth * group
    lanes = 128
    at = iota((size, lanes), 1).astype(F32).astype(BF)
    row = iota((size, 1), 0)
    level = (row // group == iota((size, depth), 1)).astype(F32).astype(BF)
    for k in range(tiles):
        times = dot(level, tt_ref[k].astype(F32).astype(BF))
        for h in range(traces // group):
            own = iota((size, traces), 1) == row % group + h * group
            code = jnp.where(own, times, 0.0).astype(BF)
            code = dot(code, jnp.ones((traces, lanes), F32).astype(BF))
            code = (code + (row % group * blocks).astype(F32)).astype(BF)
            one, zero = jnp.ones_like(code), jnp.zeros_like(code)
            pick = jnp.concatenate(
                [jnp.where(code == at + BF(i), one, zero) for i in range(0, group * blocks, lanes)],
                axis=1,
            )
            pick_ref[k * (traces // group) + h] = pick
            drop_ref[k * (traces // group) + h] = pick.astype(F32).T.astype(BF)


def by_band(band, values, bands):
    zero = jnp.zeros_like(values)
    return jnp.concatenate([jnp.where(band == BF(b), values, zero) for b in range(bands)], axis=1)


def spread(marks, first, second):
    width = marks.shape[1]
    lane = iota((width, 2 * width), 1)
    want = jnp.where(lane < width, first, second)
    return dot(marks, (iota((width, 2 * width), 0) == want).astype(F32).astype(BF)).astype(BF)


def put(ref, z, value):
    if len(ref.shape) == 4:
        ref[:, z] = value.reshape(ref.shape[0], ref.shape[2], ref.shape[3])
    else:
        ref[z] = value


def get(ref, z):
    if len(ref.shape) == 4:
        return ref[:, z].reshape(ref.shape[0] * ref.shape[2], ref.shape[3])
    return ref[z]


def rows_kernel(image_ref, tab_ref, out_ref):
    levels, width, cells = image_ref.shape
    rows = dot(image_ref[...].reshape(levels * width, cells), tab_ref[...], ((1,), (1,)))
    out_ref[...] = rows.astype(BF).reshape(out_ref.shape)


def demig(bands, first, msg_ref, rows, out_ref):
    levels, width, long = rows.shape
    block_len = long // bands
    amp = msg_ref[:, :width]
    marks = msg_ref[:, width:]
    for i in range(0, levels, 2):
        z = first + i
        both = spread(marks, z, z + 1)
        for j in range(2):
            level = jnp.concatenate(
                [rows[i + j, :, b * block_len : (b + 1) * block_len] for b in range(bands)], axis=0
            )
            weights = by_band(both[:, j * width : (j + 1) * width], amp, bands)
            put(out_ref, i + j, dot(weights, level).astype(BF))


def demig_kernel(bands, base, msg_ref, rows_ref, out_ref):
    levels = rows_ref.shape[0]
    demig(bands, base + pl.program_id(0) * levels, msg_ref, rows_ref[...], out_ref)


def whole_kernel(bands, base, msg_ref, image_ref, tab_ref, out_ref):
    levels, width, cells = image_ref.shape
    rows = dot(image_ref[...].reshape(levels * width, cells), tab_ref[...], ((1,), (1,)))
    rows = rows.astype(BF).reshape(levels, width, tab_ref.shape[0])
    demig(bands, base + pl.program_id(0) * levels, msg_ref, rows, out_ref)


def residual_kernel(depth, parts, *refs):
    place_ref, take_ref, pick_ref, drop_ref, obs_ref = refs[:5]
    recv = refs[5 : 5 + parts]
    res_ref, send_ref, pair_ref = refs[5 + parts :]
    traces, blocks, block_len = obs_ref.shape
    group = 256 // blocks
    halves = traces // group
    tiles = pick_ref.shape[0] // halves
    take = take_ref[...]
    per = depth // parts
    for z in range(depth):
        pair_ref[z] = dot(take, get(recv[z // per], z % per)).astype(BF)
    for h in range(halves):
        total = -obs_ref[h * group : (h + 1) * group].astype(F32).reshape(group * blocks, block_len)
        for k in range(tiles):
            at = slice(k * traces + h * group, k * traces + (h + 1) * group)
            part = pair_ref[:, at, :].reshape(depth * group, block_len)
            total = total + dot(drop_ref[k * halves + h], part)
        res_ref[h * group : (h + 1) * group] = total.reshape(group, blocks, block_len)
        low = total.astype(BF)
        for k in range(tiles):
            at = slice(k * traces + h * group, k * traces + (h + 1) * group)
            got = dot(pick_ref[k * halves + h], low).astype(BF)
            pair_ref[:, at, :] = got.reshape(depth, group, block_len)
    place = place_ref[...]
    for z in range(depth):
        put(send_ref, z, dot(place, pair_ref[z]).astype(BF))


def image_kernel(bands, msg_ref, blk_ref, tab_ref, out_ref, amp_ref, stack_ref):
    step = pl.program_id(0)
    levels, width, cells = out_ref.shape
    marks = msg_ref[:, width:]

    @pl.when(step == 0)
    def _():
        amp_ref[...] = msg_ref[:, :width].astype(F32).T.astype(BF)

    for i in range(0, levels, 2):
        z = step * levels + i
        both = spread(marks, z, z + 1)
        for j in range(2):
            masked = by_band(both[:, j * width : (j + 1) * width], get(blk_ref, i + j), bands)
            stack = dot(amp_ref[...], masked)
            stack_ref[(i + j) * width : (i + j + 1) * width, :] = stack.astype(BF)
    out_ref[...] = dot(stack_ref[...], tab_ref[...]).reshape(levels, width, cells)


def shards(model_image, tables, observed, aperture, traveltime, band_index, amplitude):
    devices = lax.axis_size("gx") * lax.axis_size("gy")
    depth, width_x, width_y = model_image.shape
    bands, block_len, _ = tables.shape
    traces, tile_count = aperture.shape
    blocks = observed.shape[1]
    capacity = max(2, 2 * traces * tile_count // devices)
    slots = devices * capacity
    pairs = traces * tile_count
    long = bands * block_len
    levels = 4
    aligned = capacity % 8 == 0
    groups = pairs * blocks // 256
    tables_flat = tables.reshape(long, width_y)

    def cost(flops, moved):
        return pl.CostEstimate(flops=flops, bytes_accessed=moved, transcendentals=0)

    def shape_of(count):
        if aligned:
            return (devices, count, capacity, block_len)
        return (count, slots, block_len)

    def block_of(count):
        if aligned:
            return pl.BlockSpec((devices, count, capacity, block_len), lambda z: (0, z, 0, 0))
        return pl.BlockSpec((count, slots, block_len), lambda z: (z, 0, 0))

    def exchange(x):
        if not aligned:
            x = x.reshape(-1, devices, capacity, block_len).transpose(1, 0, 2, 3)
        x = lax.all_to_all(x, ("gx", "gy"), split_axis=0, concat_axis=0, tiled=True)
        if not aligned:
            x = x.transpose(1, 0, 2, 3).reshape(-1, slots, block_len)
        return x

    message, place = pl.pallas_call(
        functools.partial(prep_kernel, devices, capacity),
        out_shape=(
            jax.ShapeDtypeStruct((slots, 2 * width_x), BF),
            jax.ShapeDtypeStruct((slots, pairs), BF),
        ),
        in_specs=[VMEM] * 3,
        out_specs=(VMEM, VMEM),
        name="prep",
    )(aperture.T, band_index.transpose(1, 2, 0), amplitude)
    got = lax.all_to_all(message, ("gx", "gy"), split_axis=0, concat_axis=0, tiled=True)

    half = depth // 2
    rows = pl.pallas_call(
        rows_kernel,
        grid=(half // levels,),
        out_shape=jax.ShapeDtypeStruct((half, width_x, long), BF),
        in_specs=[
            pl.BlockSpec((levels, width_x, width_y), lambda z: (z, 0, 0)),
            pl.BlockSpec((long, width_y), lambda z: (0, 0)),
        ],
        out_specs=pl.BlockSpec((levels, width_x, long), lambda z: (z, 0, 0)),
        cost_estimate=cost(2 * half * width_x * width_y * long, 4 * half * width_x * width_y),
        name="rows",
    )(model_image, tables_flat)
    rows = pltpu.with_memory_space_constraint(rows, pltpu.HBM)
    message_spec = pl.BlockSpec((slots, 2 * width_x), lambda z: (0, 0))
    first = pl.pallas_call(
        functools.partial(demig_kernel, bands, 0),
        grid=(half // levels,),
        out_shape=jax.ShapeDtypeStruct(shape_of(half), BF),
        in_specs=[message_spec, pl.BlockSpec((levels, width_x, long), lambda z: (z, 0, 0))],
        out_specs=block_of(levels),
        compiler_params=GRANT,
        cost_estimate=cost(2 * half * slots * width_x * long, 2 * half * width_x * long),
        name="demig",
    )(got, rows)
    back = exchange(first)
    _, image_late = lax.optimization_barrier((first, model_image))
    second = pl.pallas_call(
        functools.partial(whole_kernel, bands, half),
        grid=((depth - half) // levels,),
        out_shape=jax.ShapeDtypeStruct(shape_of(depth - half), BF),
        in_specs=[
            message_spec,
            pl.BlockSpec((levels, width_x, width_y), lambda z: (z + half // levels, 0, 0)),
            pl.BlockSpec((long, width_y), lambda z: (0, 0)),
        ],
        out_specs=block_of(levels),
        cost_estimate=cost(
            2 * (depth - half) * width_x * long * (width_y + slots), 4 * half * width_x * width_y
        ),
        name="whole",
    )(got, image_late, tables_flat)
    back_late = exchange(second)
    take, pick, drop = pl.pallas_call(
        functools.partial(codes_kernel, blocks),
        out_shape=(
            jax.ShapeDtypeStruct((pairs, slots), BF),
            jax.ShapeDtypeStruct((groups, 256, 256), BF),
            jax.ShapeDtypeStruct((groups, 256, 256), BF),
        ),
        in_specs=[VMEM, VMEM],
        out_specs=(VMEM,) * 3,
        compiler_params=GRANT,
        cost_estimate=cost(groups * 256 * 256 * 256, groups * 256 * 256 * 4),
        name="codes",
    )(place, traveltime.transpose(1, 2, 0))
    residual, outgoing = pl.pallas_call(
        functools.partial(residual_kernel, depth, 2),
        out_shape=(
            jax.ShapeDtypeStruct((traces, blocks, block_len), F32),
            jax.ShapeDtypeStruct(shape_of(depth), BF),
        ),
        in_specs=[VMEM] * 7,
        out_specs=(VMEM, VMEM),
        scratch_shapes=[pltpu.VMEM((depth, pairs, block_len), BF)],
        compiler_params=GRANT,
        cost_estimate=cost(4 * depth * slots * pairs * block_len, 4 * depth * slots * block_len),
        name="resid",
    )(place, take, pick, drop, observed, back, back_late)
    incoming = exchange(outgoing)
    gradient = pl.pallas_call(
        functools.partial(image_kernel, bands),
        grid=(depth // levels,),
        out_shape=jax.ShapeDtypeStruct((depth, width_x, width_y), F32),
        in_specs=[
            message_spec,
            block_of(levels),
            pl.BlockSpec((long, width_y), lambda z: (0, 0)),
        ],
        out_specs=pl.BlockSpec((levels, width_x, width_y), lambda z: (z, 0, 0)),
        scratch_shapes=[
            pltpu.VMEM((width_x, slots), BF),
            pltpu.VMEM((levels * width_x, long), BF),
        ],
        compiler_params=GRANT,
        cost_estimate=cost(
            2 * depth * width_x * long * (width_y + slots), 4 * depth * width_x * width_y
        ),
        name="image",
    )(got, incoming, tables_flat)
    return residual, gradient


def solution(mesh):
    both = ("gx", "gy")
    placed = (
        P(None, "gx", "gy"),
        P(),
        P(both, None, None),
        P(both, None),
        P(both, None, None),
        P(both, None, None),
        P(both, None, None),
    )
    return jax.shard_map(
        shards,
        mesh=mesh,
        in_specs=placed,
        out_specs=(P(both, None, None), P(None, "gx", "gy")),
        check_vma=False,
    )
```

```python
import functools

import jax
import jax.numpy as jnp
from jax import lax
from jax.experimental import pallas as pl
from jax.experimental.pallas import tpu as pltpu
from jax.sharding import PartitionSpec as P

BF = jnp.bfloat16
F32 = jnp.float32
GRANT = pltpu.CompilerParams(vmem_limit_bytes=20 * 1024 * 1024)
VMEM = pl.BlockSpec(memory_space=pltpu.VMEM)


def dot(a, b, dims=((1,), (0,))):
    return lax.dot_general(a, b, (dims, ((), ())), preferred_element_type=F32)


def iota(shape, axis):
    return lax.broadcasted_iota(jnp.int32, shape, axis)


def prep_kernel(devices, capacity, ap_ref, bi_ref, am_ref, msg_ref, place_ref):
    tiles, traces = ap_ref.shape
    slots = devices * capacity
    width = am_ref.shape[2]
    depth = bi_ref.shape[1]
    before = (iota((traces, traces), 0) < iota((traces, traces), 1)).astype(BF)
    base = jnp.zeros((devices, 1), F32)
    amp = jnp.zeros((slots, width), F32)
    marks = jnp.zeros((slots, width), F32)
    for k in range(tiles):
        dest = ap_ref[k : k + 1, :]
        hit = iota((devices, traces), 0) == dest
        hits = hit.astype(F32)
        rank = jnp.sum(hits * (base + dot(hits.astype(BF), before)), axis=0, keepdims=True)
        base = base + jnp.sum(hits, axis=1, keepdims=True)
        pos = dest * capacity + rank.astype(jnp.int32)
        place = (iota((slots, traces), 0) == pos).astype(F32).astype(BF)
        place_ref[:, k * traces : (k + 1) * traces] = place
        amp = amp + dot(place, am_ref[:, k, :])
        levels = jnp.concatenate(
            [bi_ref[k].astype(F32), jnp.zeros((width - depth, traces), F32)], axis=0
        ).astype(BF)
        marks = marks + dot(place, levels, ((1,), (1,)))
    msg_ref[:, :width] = amp.astype(BF)
    msg_ref[:, width:] = marks.astype(BF)


def codes_kernel(blocks, place_ref, tt_ref, take_ref, pick_ref, drop_ref):
    tiles, depth, traces = tt_ref.shape
    group = 256 // blocks
    take_ref[...] = place_ref[...].astype(F32).T.astype(BF)
    size = depth * group
    lanes = 128
    at = iota((size, lanes), 1).astype(F32).astype(BF)
    row = iota((size, 1), 0)
    level = (row // group == iota((size, depth), 1)).astype(F32).astype(BF)
    for k in range(tiles):
        times = dot(level, tt_ref[k].astype(F32).astype(BF))
        for h in range(traces // group):
            own = iota((size, traces), 1) == row % group + h * group
            code = jnp.where(own, times, 0.0).astype(BF)
            code = dot(code, jnp.ones((traces, lanes), F32).astype(BF))
            code = (code + (row % group * blocks).astype(F32)).astype(BF)
            one, zero = jnp.ones_like(code), jnp.zeros_like(code)
            pick = jnp.concatenate(
                [jnp.where(code == at + BF(i), one, zero) for i in range(0, group * blocks, lanes)],
                axis=1,
            )
            pick_ref[k * (traces // group) + h] = pick
            drop_ref[k * (traces // group) + h] = pick.astype(F32).T.astype(BF)


def by_band(band, values, bands):
    zero = jnp.zeros_like(values)
    return jnp.concatenate([jnp.where(band == BF(b), values, zero) for b in range(bands)], axis=1)


def spread(marks, first, second):
    width = marks.shape[1]
    lane = iota((width, 2 * width), 1)
    want = jnp.where(lane < width, first, second)
    return dot(marks, (iota((width, 2 * width), 0) == want).astype(F32).astype(BF)).astype(BF)


def put(ref, z, value):
    if len(ref.shape) == 4:
        ref[:, z] = value.reshape(ref.shape[0], ref.shape[2], ref.shape[3])
    else:
        ref[z] = value


def get(ref, z):
    if len(ref.shape) == 4:
        return ref[:, z].reshape(ref.shape[0] * ref.shape[2], ref.shape[3])
    return ref[z]


def rows_kernel(image_ref, tab_ref, out_ref):
    levels, width, cells = image_ref.shape
    rows = dot(image_ref[...].reshape(levels * width, cells), tab_ref[...], ((1,), (1,)))
    out_ref[...] = rows.astype(BF).reshape(out_ref.shape)


def demig_kernel(bands, msg_ref, rows_ref, out_ref):
    levels, width, long = rows_ref.shape
    block_len = long // bands
    amp = msg_ref[:, :width]
    marks = msg_ref[:, width:]
    for i in range(0, levels, 2):
        z = pl.program_id(0) * levels + i
        both = spread(marks, z, z + 1)
        for j in range(2):
            level = jnp.concatenate(
                [rows_ref[i + j, :, b * block_len : (b + 1) * block_len] for b in range(bands)],
                axis=0,
            )
            weights = by_band(both[:, j * width : (j + 1) * width], amp, bands)
            put(out_ref, i + j, dot(weights, level).astype(BF))


def residual_kernel(
    place_ref, take_ref, pick_ref, drop_ref, obs_ref, recv_ref, res_ref, send_ref, pair_ref
):
    depth = pair_ref.shape[0]
    traces, blocks, block_len = obs_ref.shape
    group = 256 // blocks
    halves = traces // group
    tiles = pick_ref.shape[0] // halves
    take = take_ref[...]
    for z in range(depth):
        pair_ref[z] = dot(take, get(recv_ref, z)).astype(BF)
    for h in range(halves):
        total = -obs_ref[h * group : (h + 1) * group].astype(F32).reshape(group * blocks, block_len)
        for k in range(tiles):
            at = slice(k * traces + h * group, k * traces + (h + 1) * group)
            part = pair_ref[:, at, :].reshape(depth * group, block_len)
            total = total + dot(drop_ref[k * halves + h], part)
        res_ref[h * group : (h + 1) * group] = total.reshape(group, blocks, block_len)
        low = total.astype(BF)
        for k in range(tiles):
            at = slice(k * traces + h * group, k * traces + (h + 1) * group)
            got = dot(pick_ref[k * halves + h], low).astype(BF)
            pair_ref[:, at, :] = got.reshape(depth, group, block_len)
    place = place_ref[...]
    for z in range(depth):
        put(send_ref, z, dot(place, pair_ref[z]).astype(BF))


def image_kernel(bands, msg_ref, blk_ref, tab_ref, out_ref, amp_ref, stack_ref):
    step = pl.program_id(0)
    levels, width, cells = out_ref.shape
    marks = msg_ref[:, width:]

    @pl.when(step == 0)
    def _():
        amp_ref[...] = msg_ref[:, :width].astype(F32).T.astype(BF)

    for i in range(0, levels, 2):
        z = step * levels + i
        both = spread(marks, z, z + 1)
        for j in range(2):
            masked = by_band(both[:, j * width : (j + 1) * width], get(blk_ref, i + j), bands)
            stack = dot(amp_ref[...], masked)
            stack_ref[(i + j) * width : (i + j + 1) * width, :] = stack.astype(BF)
    out_ref[...] = dot(stack_ref[...], tab_ref[...]).reshape(levels, width, cells)


def shards(model_image, tables, observed, aperture, traveltime, band_index, amplitude):
    devices = lax.axis_size("gx") * lax.axis_size("gy")
    depth, width_x, width_y = model_image.shape
    bands, block_len, _ = tables.shape
    traces, tile_count = aperture.shape
    blocks = observed.shape[1]
    capacity = max(2, 2 * traces * tile_count // devices)
    slots = devices * capacity
    pairs = traces * tile_count
    long = bands * block_len
    levels = 4
    aligned = capacity % 8 == 0
    groups = pairs * blocks // 256
    tables_flat = tables.reshape(long, width_y)

    def cost(flops, moved):
        return pl.CostEstimate(flops=flops, bytes_accessed=moved, transcendentals=0)

    def shape_of(count):
        if aligned:
            return (devices, count, capacity, block_len)
        return (count, slots, block_len)

    def block_of(count):
        if aligned:
            return pl.BlockSpec((devices, count, capacity, block_len), lambda z: (0, z, 0, 0))
        return pl.BlockSpec((count, slots, block_len), lambda z: (z, 0, 0))

    def exchange(x):
        if not aligned:
            x = x.reshape(-1, devices, capacity, block_len).transpose(1, 0, 2, 3)
        x = lax.all_to_all(x, ("gx", "gy"), split_axis=0, concat_axis=0, tiled=True)
        if not aligned:
            x = x.transpose(1, 0, 2, 3).reshape(-1, slots, block_len)
        return x

    message, place = pl.pallas_call(
        functools.partial(prep_kernel, devices, capacity),
        out_shape=(
            jax.ShapeDtypeStruct((slots, 2 * width_x), BF),
            jax.ShapeDtypeStruct((slots, pairs), BF),
        ),
        in_specs=[VMEM] * 3,
        out_specs=(VMEM, VMEM),
        name="prep",
    )(aperture.T, band_index.transpose(1, 2, 0), amplitude)
    got = lax.all_to_all(message, ("gx", "gy"), split_axis=0, concat_axis=0, tiled=True)

    rows = pl.pallas_call(
        rows_kernel,
        grid=(depth // levels,),
        out_shape=jax.ShapeDtypeStruct((depth, width_x, long), BF),
        in_specs=[
            pl.BlockSpec((levels, width_x, width_y), lambda z: (z, 0, 0)),
            pl.BlockSpec((long, width_y), lambda z: (0, 0)),
        ],
        out_specs=pl.BlockSpec((levels, width_x, long), lambda z: (z, 0, 0)),
        cost_estimate=cost(2 * depth * width_x * width_y * long, 4 * depth * width_x * width_y),
        name="rows",
    )(model_image, tables_flat)
    rows = pltpu.with_memory_space_constraint(rows, pltpu.HBM)
    message_spec = pl.BlockSpec((slots, 2 * width_x), lambda z: (0, 0))
    partials = pl.pallas_call(
        functools.partial(demig_kernel, bands),
        grid=(depth // levels,),
        out_shape=jax.ShapeDtypeStruct(shape_of(depth), BF),
        in_specs=[message_spec, pl.BlockSpec((levels, width_x, long), lambda z: (z, 0, 0))],
        out_specs=block_of(levels),
        compiler_params=GRANT,
        cost_estimate=cost(2 * depth * slots * width_x * long, 2 * depth * width_x * long),
        name="demig",
    )(got, rows)
    returned = exchange(partials)
    take, pick, drop = pl.pallas_call(
        functools.partial(codes_kernel, blocks),
        out_shape=(
            jax.ShapeDtypeStruct((pairs, slots), BF),
            jax.ShapeDtypeStruct((groups, 256, 256), BF),
            jax.ShapeDtypeStruct((groups, 256, 256), BF),
        ),
        in_specs=[VMEM, VMEM],
        out_specs=(VMEM,) * 3,
        compiler_params=GRANT,
        cost_estimate=cost(groups * 256 * 256 * 256, groups * 256 * 256 * 4),
        name="codes",
    )(place, traveltime.transpose(1, 2, 0))
    residual, outgoing = pl.pallas_call(
        residual_kernel,
        out_shape=(
            jax.ShapeDtypeStruct((traces, blocks, block_len), F32),
            jax.ShapeDtypeStruct(shape_of(depth), BF),
        ),
        in_specs=[VMEM] * 6,
        out_specs=(VMEM, VMEM),
        scratch_shapes=[pltpu.VMEM((depth, pairs, block_len), BF)],
        compiler_params=GRANT,
        cost_estimate=cost(4 * depth * slots * pairs * block_len, 4 * depth * slots * block_len),
        name="resid",
    )(place, take, pick, drop, observed, returned)
    incoming = exchange(outgoing)
    gradient = pl.pallas_call(
        functools.partial(image_kernel, bands),
        grid=(depth // levels,),
        out_shape=jax.ShapeDtypeStruct((depth, width_x, width_y), F32),
        in_specs=[
            message_spec,
            block_of(levels),
            pl.BlockSpec((long, width_y), lambda z: (0, 0)),
        ],
        out_specs=pl.BlockSpec((levels, width_x, width_y), lambda z: (z, 0, 0)),
        scratch_shapes=[
            pltpu.VMEM((width_x, slots), BF),
            pltpu.VMEM((levels * width_x, long), BF),
        ],
        compiler_params=GRANT,
        cost_estimate=cost(
            2 * depth * width_x * long * (width_y + slots), 4 * depth * width_x * width_y
        ),
        name="image",
    )(got, incoming, tables_flat)
    return residual, gradient


def solution(mesh):
    both = ("gx", "gy")
    placed = (
        P(None, "gx", "gy"),
        P(),
        P(both, None, None),
        P(both, None),
        P(both, None, None),
        P(both, None, None),
        P(both, None, None),
    )
    return jax.shard_map(
        shards,
        mesh=mesh,
        in_specs=placed,
        out_specs=(P(both, None, None), P(None, "gx", "gy")),
        check_vma=False,
    )
```

```python
import functools

import jax
import jax.numpy as jnp
from jax import lax
from jax.experimental import pallas as pl
from jax.experimental.pallas import tpu as pltpu
from jax.sharding import PartitionSpec as P

BF = jnp.bfloat16
F32 = jnp.float32
GRANT = pltpu.CompilerParams(vmem_limit_bytes=20 * 1024 * 1024)
VMEM = pl.BlockSpec(memory_space=pltpu.VMEM)


def dot(a, b, dims=((1,), (0,))):
    return lax.dot_general(a, b, (dims, ((), ())), preferred_element_type=F32)


def iota(shape, axis):
    return lax.broadcasted_iota(jnp.int32, shape, axis)


def prep_kernel(devices, capacity, ap_ref, bi_ref, am_ref, msg_ref, place_ref):
    tiles, traces = ap_ref.shape
    slots = devices * capacity
    width = am_ref.shape[2]
    depth = bi_ref.shape[1]
    before = (iota((traces, traces), 0) < iota((traces, traces), 1)).astype(BF)
    base = jnp.zeros((devices, 1), F32)
    amp = jnp.zeros((slots, width), F32)
    marks = jnp.zeros((slots, width), F32)
    for k in range(tiles):
        dest = ap_ref[k : k + 1, :]
        hit = iota((devices, traces), 0) == dest
        hits = hit.astype(F32)
        rank = jnp.sum(hits * (base + dot(hits.astype(BF), before)), axis=0, keepdims=True)
        base = base + jnp.sum(hits, axis=1, keepdims=True)
        pos = dest * capacity + rank.astype(jnp.int32)
        place = (iota((slots, traces), 0) == pos).astype(F32).astype(BF)
        place_ref[:, k * traces : (k + 1) * traces] = place
        amp = amp + dot(place, am_ref[:, k, :])
        levels = jnp.concatenate(
            [bi_ref[k].astype(F32), jnp.zeros((width - depth, traces), F32)], axis=0
        ).astype(BF)
        marks = marks + dot(place, levels, ((1,), (1,)))
    msg_ref[:, :width] = amp.astype(BF)
    msg_ref[:, width:] = marks.astype(BF)


def codes_kernel(
    blocks, msg_ref, place_ref, tt_ref, take_ref, pick_ref, drop_ref, amp_ref, band_ref
):
    tiles, depth, traces = tt_ref.shape
    group = 256 // blocks
    width = amp_ref.shape[0]
    amp_ref[...] = msg_ref[:, :width].astype(F32).T.astype(BF)
    for z in range(0, depth, 2):
        both = spread(msg_ref[:, width:], z, z + 1)
        band_ref[z] = both[:, :width]
        band_ref[z + 1] = both[:, width:]
    take_ref[...] = place_ref[...].astype(F32).T.astype(BF)
    size = depth * group
    lanes = 128
    at = iota((size, lanes), 1).astype(F32).astype(BF)
    row = iota((size, 1), 0)
    level = (row // group == iota((size, depth), 1)).astype(F32).astype(BF)
    for k in range(tiles):
        times = dot(level, tt_ref[k].astype(F32).astype(BF))
        for h in range(traces // group):
            own = iota((size, traces), 1) == row % group + h * group
            code = jnp.where(own, times, 0.0).astype(BF)
            code = dot(code, jnp.ones((traces, lanes), F32).astype(BF))
            code = (code + (row % group * blocks).astype(F32)).astype(BF)
            one, zero = jnp.ones_like(code), jnp.zeros_like(code)
            pick = jnp.concatenate(
                [jnp.where(code == at + BF(i), one, zero) for i in range(0, group * blocks, lanes)],
                axis=1,
            )
            pick_ref[k * (traces // group) + h] = pick
            drop_ref[k * (traces // group) + h] = pick.astype(F32).T.astype(BF)


def by_band(band, values, bands):
    zero = jnp.zeros_like(values)
    return jnp.concatenate([jnp.where(band == BF(b), values, zero) for b in range(bands)], axis=1)


def spread(marks, first, second):
    width = marks.shape[1]
    lane = iota((width, 2 * width), 1)
    want = jnp.where(lane < width, first, second)
    return dot(marks, (iota((width, 2 * width), 0) == want).astype(F32).astype(BF)).astype(BF)


def put(ref, z, value):
    if len(ref.shape) == 4:
        ref[:, z] = value.reshape(ref.shape[0], ref.shape[2], ref.shape[3])
    else:
        ref[z] = value


def get(ref, z):
    if len(ref.shape) == 4:
        return ref[:, z].reshape(ref.shape[0] * ref.shape[2], ref.shape[3])
    return ref[z]


def rows_kernel(image_ref, tab_ref, out_ref):
    levels, width, cells = image_ref.shape
    rows = dot(image_ref[...].reshape(levels * width, cells), tab_ref[...], ((1,), (1,)))
    out_ref[...] = rows.astype(BF).reshape(out_ref.shape)


def demig_kernel(bands, msg_ref, rows_ref, out_ref):
    levels, width, long = rows_ref.shape
    block_len = long // bands
    amp = msg_ref[:, :width]
    shift = (width - pl.program_id(0) * levels) % width
    marks = pltpu.roll(msg_ref[:, width:].astype(F32), shift, 1)
    for i in range(levels):
        band = jnp.broadcast_to(marks[:, i : i + 1], amp.shape).astype(BF)
        rows = jnp.concatenate(
            [rows_ref[i, :, b * block_len : (b + 1) * block_len] for b in range(bands)], axis=0
        )
        put(out_ref, i, dot(by_band(band, amp, bands), rows).astype(BF))


def residual_kernel(
    place_ref, take_ref, pick_ref, drop_ref, obs_ref, recv_ref, res_ref, send_ref, pair_ref
):
    depth = pair_ref.shape[0]
    traces, blocks, block_len = obs_ref.shape
    group = 256 // blocks
    halves = traces // group
    tiles = pick_ref.shape[0] // halves
    take = take_ref[...]
    for z in range(0, depth, 2):
        two = dot(take, jnp.concatenate([get(recv_ref, z), get(recv_ref, z + 1)], axis=1)).astype(BF)
        pair_ref[z] = two[:, :block_len]
        pair_ref[z + 1] = two[:, block_len:]
    for h in range(halves):
        total = -obs_ref[h * group : (h + 1) * group].astype(F32).reshape(group * blocks, block_len)
        for k in range(tiles):
            at = slice(k * traces + h * group, k * traces + (h + 1) * group)
            part = pair_ref[:, at, :].reshape(depth * group, block_len)
            total = total + dot(drop_ref[k * halves + h], part)
        res_ref[h * group : (h + 1) * group] = total.reshape(group, blocks, block_len)
        low = total.astype(BF)
        for k in range(tiles):
            at = slice(k * traces + h * group, k * traces + (h + 1) * group)
            got = dot(pick_ref[k * halves + h], low).astype(BF)
            pair_ref[:, at, :] = got.reshape(depth, group, block_len)
    place = place_ref[...]
    for z in range(0, depth, 2):
        two = dot(place, jnp.concatenate([pair_ref[z], pair_ref[z + 1]], axis=1)).astype(BF)
        put(send_ref, z, two[:, :block_len])
        put(send_ref, z + 1, two[:, block_len:])


def image_kernel(bands, amp_ref, band_ref, blk_ref, tab_ref, out_ref, stack_ref):
    levels, width, cells = out_ref.shape
    for i in range(levels):
        masked = by_band(band_ref[i], get(blk_ref, i), bands)
        stack_ref[i * width : (i + 1) * width, :] = dot(amp_ref[...], masked).astype(BF)
    out_ref[...] = dot(stack_ref[...], tab_ref[...]).reshape(levels, width, cells)


def shards(model_image, tables, observed, aperture, traveltime, band_index, amplitude):
    devices = lax.axis_size("gx") * lax.axis_size("gy")
    depth, width_x, width_y = model_image.shape
    bands, block_len, _ = tables.shape
    traces, tile_count = aperture.shape
    blocks = observed.shape[1]
    capacity = max(2, 2 * traces * tile_count // devices)
    slots = devices * capacity
    pairs = traces * tile_count
    long = bands * block_len
    levels = 4
    aligned = capacity % 8 == 0
    groups = pairs * blocks // 256
    tables_flat = tables.reshape(long, width_y)

    def cost(flops, moved):
        return pl.CostEstimate(flops=flops, bytes_accessed=moved, transcendentals=0)

    def shape_of(count):
        if aligned:
            return (devices, count, capacity, block_len)
        return (count, slots, block_len)

    def block_of(count):
        if aligned:
            return pl.BlockSpec((devices, count, capacity, block_len), lambda z: (0, z, 0, 0))
        return pl.BlockSpec((count, slots, block_len), lambda z: (z, 0, 0))

    def exchange(x):
        if not aligned:
            x = x.reshape(-1, devices, capacity, block_len).transpose(1, 0, 2, 3)
        x = lax.all_to_all(x, ("gx", "gy"), split_axis=0, concat_axis=0, tiled=True)
        if not aligned:
            x = x.transpose(1, 0, 2, 3).reshape(-1, slots, block_len)
        return x

    message, place = pl.pallas_call(
        functools.partial(prep_kernel, devices, capacity),
        out_shape=(
            jax.ShapeDtypeStruct((slots, 2 * width_x), BF),
            jax.ShapeDtypeStruct((slots, pairs), BF),
        ),
        in_specs=[VMEM] * 3,
        out_specs=(VMEM, VMEM),
        name="prep",
    )(aperture.T, band_index.transpose(1, 2, 0), amplitude)
    got = lax.all_to_all(message, ("gx", "gy"), split_axis=0, concat_axis=0, tiled=True)

    rows = pl.pallas_call(
        rows_kernel,
        grid=(depth // levels,),
        out_shape=jax.ShapeDtypeStruct((depth, width_x, long), BF),
        in_specs=[
            pl.BlockSpec((levels, width_x, width_y), lambda z: (z, 0, 0)),
            pl.BlockSpec((long, width_y), lambda z: (0, 0)),
        ],
        out_specs=pl.BlockSpec((levels, width_x, long), lambda z: (z, 0, 0)),
        cost_estimate=cost(2 * depth * width_x * width_y * long, 4 * depth * width_x * width_y),
        name="rows",
    )(model_image, tables_flat)
    rows = pltpu.with_memory_space_constraint(rows, pltpu.HBM)
    partials = pl.pallas_call(
        functools.partial(demig_kernel, bands),
        grid=(depth // (2 * levels),),
        out_shape=jax.ShapeDtypeStruct(shape_of(depth), BF),
        in_specs=[
            pl.BlockSpec((slots, 2 * width_x), lambda z: (0, 0)),
            pl.BlockSpec((2 * levels, width_x, long), lambda z: (z, 0, 0)),
        ],
        out_specs=block_of(2 * levels),
        compiler_params=GRANT,
        cost_estimate=cost(2 * depth * slots * width_x * long, 2 * depth * width_x * long),
        name="demig",
    )(got, rows)
    returned = exchange(partials)
    take, pick, drop, turned, spread_bands = pl.pallas_call(
        functools.partial(codes_kernel, blocks),
        out_shape=(
            jax.ShapeDtypeStruct((pairs, slots), BF),
            jax.ShapeDtypeStruct((groups, 256, 256), BF),
            jax.ShapeDtypeStruct((groups, 256, 256), BF),
            jax.ShapeDtypeStruct((width_x, slots), BF),
            jax.ShapeDtypeStruct((depth, slots, width_x), BF),
        ),
        in_specs=[VMEM] * 3,
        out_specs=(VMEM,) * 5,
        compiler_params=GRANT,
        cost_estimate=cost(groups * 256 * 256 * 256, groups * 256 * 256 * 4),
        name="codes",
    )(got, place, traveltime.transpose(1, 2, 0))
    residual, outgoing = pl.pallas_call(
        residual_kernel,
        out_shape=(
            jax.ShapeDtypeStruct((traces, blocks, block_len), F32),
            jax.ShapeDtypeStruct(shape_of(depth), BF),
        ),
        in_specs=[VMEM] * 6,
        out_specs=(VMEM, VMEM),
        scratch_shapes=[pltpu.VMEM((depth, pairs, block_len), BF)],
        compiler_params=GRANT,
        cost_estimate=cost(4 * depth * slots * pairs * block_len, 4 * depth * slots * block_len),
        name="resid",
    )(place, take, pick, drop, observed, returned)
    incoming = exchange(outgoing)
    gradient = pl.pallas_call(
        functools.partial(image_kernel, bands),
        grid=(depth // levels,),
        out_shape=jax.ShapeDtypeStruct((depth, width_x, width_y), F32),
        in_specs=[
            pl.BlockSpec((width_x, slots), lambda z: (0, 0)),
            pl.BlockSpec((levels, slots, width_x), lambda z: (z, 0, 0)),
            block_of(levels),
            pl.BlockSpec((long, width_y), lambda z: (0, 0)),
        ],
        out_specs=pl.BlockSpec((levels, width_x, width_y), lambda z: (z, 0, 0)),
        scratch_shapes=[pltpu.VMEM((levels * width_x, long), BF)],
        compiler_params=GRANT,
        cost_estimate=cost(
            2 * depth * width_x * long * (width_y + slots), 4 * depth * width_x * width_y
        ),
        name="image",
    )(turned, spread_bands, incoming, tables_flat)
    return residual, gradient


def solution(mesh):
    both = ("gx", "gy")
    placed = (
        P(None, "gx", "gy"),
        P(),
        P(both, None, None),
        P(both, None),
        P(both, None, None),
        P(both, None, None),
        P(both, None, None),
    )
    return jax.shard_map(
        shards,
        mesh=mesh,
        in_specs=placed,
        out_specs=(P(both, None, None), P(None, "gx", "gy")),
        check_vma=False,
    )
```

```python
import functools

import jax
import jax.numpy as jnp
from jax import lax
from jax.experimental import pallas as pl
from jax.experimental.pallas import tpu as pltpu
from jax.sharding import PartitionSpec as P

BF = jnp.bfloat16
F32 = jnp.float32
GRANT = pltpu.CompilerParams(vmem_limit_bytes=20 * 1024 * 1024)
ANY = pl.BlockSpec(memory_space=pl.ANY)
VMEM = pl.BlockSpec(memory_space=pltpu.VMEM)


def dot(a, b, dims=((1,), (0,))):
    return lax.dot_general(a, b, (dims, ((), ())), preferred_element_type=F32)


def iota(shape, axis):
    return lax.broadcasted_iota(jnp.int32, shape, axis)


def prep_kernel(devices, capacity, ap_ref, bi_ref, am_ref, msg_ref, place_ref):
    tiles, traces = ap_ref.shape
    slots = devices * capacity
    width = am_ref.shape[2]
    depth = bi_ref.shape[1]
    before = (iota((traces, traces), 0) < iota((traces, traces), 1)).astype(BF)
    base = jnp.zeros((devices, 1), F32)
    amp = jnp.zeros((slots, width), F32)
    marks = jnp.zeros((slots, width), F32)
    for k in range(tiles):
        dest = ap_ref[k : k + 1, :]
        hit = iota((devices, traces), 0) == dest
        hits = hit.astype(F32)
        rank = jnp.sum(hits * (base + dot(hits.astype(BF), before)), axis=0, keepdims=True)
        base = base + jnp.sum(hits, axis=1, keepdims=True)
        pos = dest * capacity + rank.astype(jnp.int32)
        place = (iota((slots, traces), 0) == pos).astype(F32).astype(BF)
        place_ref[:, k * traces : (k + 1) * traces] = place
        amp = amp + dot(place, am_ref[:, k, :])
        levels = jnp.concatenate(
            [bi_ref[k].astype(F32), jnp.zeros((width - depth, traces), F32)], axis=0
        ).astype(BF)
        marks = marks + dot(place, levels, ((1,), (1,)))
    msg_ref[:, :width] = amp.astype(BF)
    msg_ref[:, width:] = marks.astype(BF)


def codes_kernel(
    blocks, msg_ref, place_ref, tt_ref, take_ref, pick_ref, drop_ref, amp_ref, band_ref
):
    tiles, depth, traces = tt_ref.shape
    group = 256 // blocks
    width = amp_ref.shape[0]
    amp_ref[...] = msg_ref[:, :width].astype(F32).T.astype(BF)
    for z in range(0, depth, 2):
        both = spread(msg_ref[:, width:], z, z + 1)
        band_ref[z] = both[:, :width]
        band_ref[z + 1] = both[:, width:]
    take_ref[...] = place_ref[...].astype(F32).T.astype(BF)
    size = depth * group
    lanes = 128
    at = iota((size, lanes), 1).astype(F32).astype(BF)
    row = iota((size, 1), 0)
    level = (row // group == iota((size, depth), 1)).astype(F32).astype(BF)
    for k in range(tiles):
        times = dot(level, tt_ref[k].astype(F32).astype(BF))
        for h in range(traces // group):
            own = iota((size, traces), 1) == row % group + h * group
            code = jnp.where(own, times, 0.0).astype(BF)
            code = dot(code, jnp.ones((traces, lanes), F32).astype(BF))
            code = (code + (row % group * blocks).astype(F32)).astype(BF)
            one, zero = jnp.ones_like(code), jnp.zeros_like(code)
            pick = jnp.concatenate(
                [jnp.where(code == at + BF(i), one, zero) for i in range(0, group * blocks, lanes)],
                axis=1,
            )
            pick_ref[k * (traces // group) + h] = pick
            drop_ref[k * (traces // group) + h] = pick.astype(F32).T.astype(BF)


def by_band(band, values, bands):
    zero = jnp.zeros_like(values)
    return jnp.concatenate([jnp.where(band == BF(b), values, zero) for b in range(bands)], axis=1)


def spread(marks, first, second):
    width = marks.shape[1]
    lane = iota((width, 2 * width), 1)
    want = jnp.where(lane < width, first, second)
    return dot(marks, (iota((width, 2 * width), 0) == want).astype(F32).astype(BF)).astype(BF)


def put(ref, z, value):
    if len(ref.shape) == 4:
        ref[:, z] = value.reshape(ref.shape[0], ref.shape[2], ref.shape[3])
    else:
        ref[z] = value


def get(ref, z):
    if len(ref.shape) == 4:
        return ref[:, z].reshape(ref.shape[0] * ref.shape[2], ref.shape[3])
    return ref[z]


def rows_kernel(
    per, cols, image_hbm, tab_hbm, out_hbm, image_ref, tab_ref, out_ref, image_sem, tab_sem, out_sem
):
    depth, width, cells = image_ref.shape
    pieces, strips = depth // per, tab_ref.shape[0] // cols

    def image_copy(m):
        at = pl.ds(m * per, per)
        return pltpu.make_async_copy(image_hbm.at[at], image_ref.at[at], image_sem.at[m])

    def tab_copy(n):
        at = pl.ds(n * cols, cols)
        return pltpu.make_async_copy(tab_hbm.at[at], tab_ref.at[at], tab_sem.at[n])

    tab_copy(0).start()
    for m in range(pieces):
        image_copy(m).start()
    for n in range(1, strips):
        tab_copy(n).start()
    sent = []
    for n in range(strips):
        tab_copy(n).wait()
        strip = tab_ref[n * cols : (n + 1) * cols, :]
        for m in range(pieces):
            if n == 0:
                image_copy(m).wait()
            levels = image_ref[m * per : (m + 1) * per].reshape(per * width, cells)
            rows = dot(levels, strip, ((1,), (1,))).astype(BF)
            out_ref[m * per : (m + 1) * per, :, n * cols : (n + 1) * cols] = rows.reshape(
                per, width, cols
            )
            at = (pl.ds(m * per, per), slice(None), pl.ds(n * cols, cols))
            copy = pltpu.make_async_copy(
                out_ref.at[at], out_hbm.at[at], out_sem.at[n * pieces + m]
            )
            copy.start()
            sent.append(copy)
    for copy in sent:
        copy.wait()


def demig_kernel(bands, per, msg_ref, rows_hbm, out_ref, rows_ref, sem):
    depth, width, long = rows_ref.shape
    block_len = long // bands
    pieces = depth // per

    def rows_copy(m):
        at = pl.ds(m * per, per)
        return pltpu.make_async_copy(rows_hbm.at[at], rows_ref.at[at], sem.at[m])

    for m in range(pieces):
        rows_copy(m).start()
    amp = msg_ref[:, :width]
    marks = msg_ref[:, width:].astype(F32)
    for m in range(pieces):
        rows_copy(m).wait()
        for z in range(m * per, (m + 1) * per):
            band = jnp.broadcast_to(marks[:, z : z + 1], amp.shape).astype(BF)
            rows = jnp.concatenate(
                [rows_ref[z, :, b * block_len : (b + 1) * block_len] for b in range(bands)], axis=0
            )
            put(out_ref, z, dot(by_band(band, amp, bands), rows).astype(BF))


def residual_kernel(
    place_ref, take_ref, pick_ref, drop_ref, obs_ref, recv_ref, res_ref, send_ref, pair_ref
):
    depth = pair_ref.shape[0]
    traces, blocks, block_len = obs_ref.shape
    group = 256 // blocks
    halves = traces // group
    tiles = pick_ref.shape[0] // halves
    take = take_ref[...]
    for z in range(0, depth, 2):
        two = dot(take, jnp.concatenate([get(recv_ref, z), get(recv_ref, z + 1)], axis=1)).astype(BF)
        pair_ref[z] = two[:, :block_len]
        pair_ref[z + 1] = two[:, block_len:]
    for h in range(halves):
        total = -obs_ref[h * group : (h + 1) * group].astype(F32).reshape(group * blocks, block_len)
        for k in range(tiles):
            at = slice(k * traces + h * group, k * traces + (h + 1) * group)
            part = pair_ref[:, at, :].reshape(depth * group, block_len)
            total = total + dot(drop_ref[k * halves + h], part)
        res_ref[h * group : (h + 1) * group] = total.reshape(group, blocks, block_len)
        low = total.astype(BF)
        for k in range(tiles):
            at = slice(k * traces + h * group, k * traces + (h + 1) * group)
            got = dot(pick_ref[k * halves + h], low).astype(BF)
            pair_ref[:, at, :] = got.reshape(depth, group, block_len)
    place = place_ref[...]
    for z in range(0, depth, 2):
        two = dot(place, jnp.concatenate([pair_ref[z], pair_ref[z + 1]], axis=1)).astype(BF)
        put(send_ref, z, two[:, :block_len])
        put(send_ref, z + 1, two[:, block_len:])


def image_kernel(
    bands, per, amp_ref, band_ref, blk_ref, tab_ref, out_hbm, stack_ref, out_ref, sem
):
    depth, width, cells = out_ref.shape
    sent = []
    for m in range(depth // per):
        for z in range(m * per, (m + 1) * per):
            masked = by_band(band_ref[z], get(blk_ref, z), bands)
            stack_ref[z * width : (z + 1) * width, :] = dot(amp_ref[...], masked).astype(BF)
        stack = stack_ref[m * per * width : (m + 1) * per * width, :]
        out_ref[m * per : (m + 1) * per] = dot(stack, tab_ref[...]).reshape(per, width, cells)
        at = pl.ds(m * per, per)
        copy = pltpu.make_async_copy(out_ref.at[at], out_hbm.at[at], sem.at[m])
        copy.start()
        sent.append(copy)
    for copy in sent:
        copy.wait()


def shards(model_image, tables, observed, aperture, traveltime, band_index, amplitude):
    devices = lax.axis_size("gx") * lax.axis_size("gy")
    depth, width_x, width_y = model_image.shape
    bands, block_len, _ = tables.shape
    traces, tile_count = aperture.shape
    blocks = observed.shape[1]
    capacity = max(2, 2 * traces * tile_count // devices)
    slots = devices * capacity
    pairs = traces * tile_count
    long = bands * block_len
    aligned = capacity % 8 == 0
    groups = pairs * blocks // 256
    tables_flat = tables.reshape(long, width_y)

    def cost(flops, moved):
        return pl.CostEstimate(flops=flops, bytes_accessed=moved, transcendentals=0)

    def shape_of(count):
        if aligned:
            return (devices, count, capacity, block_len)
        return (count, slots, block_len)

    def exchange(x):
        if not aligned:
            x = x.reshape(-1, devices, capacity, block_len).transpose(1, 0, 2, 3)
        x = lax.all_to_all(x, ("gx", "gy"), split_axis=0, concat_axis=0, tiled=True)
        if not aligned:
            x = x.transpose(1, 0, 2, 3).reshape(-1, slots, block_len)
        return x

    message, place = pl.pallas_call(
        functools.partial(prep_kernel, devices, capacity),
        out_shape=(
            jax.ShapeDtypeStruct((slots, 2 * width_x), BF),
            jax.ShapeDtypeStruct((slots, pairs), BF),
        ),
        in_specs=[VMEM] * 3,
        out_specs=(VMEM, VMEM),
        name="prep",
    )(aperture.T, band_index.transpose(1, 2, 0), amplitude)
    got = lax.all_to_all(message, ("gx", "gy"), split_axis=0, concat_axis=0, tiled=True)

    per, cols = depth // 2, long // 2
    rows = pl.pallas_call(
        functools.partial(rows_kernel, per, cols),
        out_shape=jax.ShapeDtypeStruct((depth, width_x, long), BF),
        in_specs=[ANY, ANY],
        out_specs=ANY,
        scratch_shapes=[
            pltpu.VMEM((depth, width_x, width_y), BF),
            pltpu.VMEM((long, width_y), BF),
            pltpu.VMEM((depth, width_x, long), BF),
            pltpu.SemaphoreType.DMA((depth // per,)),
            pltpu.SemaphoreType.DMA((long // cols,)),
            pltpu.SemaphoreType.DMA((depth // per * (long // cols),)),
        ],
        cost_estimate=cost(2 * depth * width_x * width_y * long, 4 * depth * width_x * width_y),
        name="rows",
    )(model_image, tables_flat)
    rows = pltpu.with_memory_space_constraint(rows, pltpu.HBM)
    per = 4
    partials = pl.pallas_call(
        functools.partial(demig_kernel, bands, per),
        out_shape=jax.ShapeDtypeStruct(shape_of(depth), BF),
        in_specs=[VMEM, ANY],
        out_specs=VMEM,
        scratch_shapes=[
            pltpu.VMEM((depth, width_x, long), BF),
            pltpu.SemaphoreType.DMA((depth // per,)),
        ],
        compiler_params=GRANT,
        cost_estimate=cost(2 * depth * slots * width_x * long, 2 * depth * width_x * long),
        name="demig",
    )(got, rows)
    returned = exchange(partials)
    take, pick, drop, turned, spread_bands = pl.pallas_call(
        functools.partial(codes_kernel, blocks),
        out_shape=(
            jax.ShapeDtypeStruct((pairs, slots), BF),
            jax.ShapeDtypeStruct((groups, 256, 256), BF),
            jax.ShapeDtypeStruct((groups, 256, 256), BF),
            jax.ShapeDtypeStruct((width_x, slots), BF),
            jax.ShapeDtypeStruct((depth, slots, width_x), BF),
        ),
        in_specs=[VMEM] * 3,
        out_specs=(VMEM,) * 5,
        compiler_params=GRANT,
        cost_estimate=cost(groups * 256 * 256 * 256, groups * 256 * 256 * 4),
        name="codes",
    )(got, place, traveltime.transpose(1, 2, 0))
    residual, outgoing = pl.pallas_call(
        residual_kernel,
        out_shape=(
            jax.ShapeDtypeStruct((traces, blocks, block_len), F32),
            jax.ShapeDtypeStruct(shape_of(depth), BF),
        ),
        in_specs=[VMEM] * 6,
        out_specs=(VMEM, VMEM),
        scratch_shapes=[pltpu.VMEM((depth, pairs, block_len), BF)],
        compiler_params=GRANT,
        cost_estimate=cost(4 * depth * slots * pairs * block_len, 4 * depth * slots * block_len),
        name="resid",
    )(place, take, pick, drop, observed, returned)
    incoming = exchange(outgoing)
    per = 2
    gradient = pl.pallas_call(
        functools.partial(image_kernel, bands, per),
        out_shape=jax.ShapeDtypeStruct((depth, width_x, width_y), F32),
        in_specs=[VMEM] * 4,
        out_specs=ANY,
        scratch_shapes=[
            pltpu.VMEM((depth * width_x, long), BF),
            pltpu.VMEM((depth, width_x, width_y), F32),
            pltpu.SemaphoreType.DMA((depth // per,)),
        ],
        compiler_params=pltpu.CompilerParams(vmem_limit_bytes=32 * 1024 * 1024),
        cost_estimate=cost(
            2 * depth * width_x * long * (width_y + slots), 4 * depth * width_x * width_y
        ),
        name="image",
    )(turned, spread_bands, incoming, tables_flat)
    return residual, gradient


def solution(mesh):
    both = ("gx", "gy")
    placed = (
        P(None, "gx", "gy"),
        P(),
        P(both, None, None),
        P(both, None),
        P(both, None, None),
        P(both, None, None),
        P(both, None, None),
    )
    return jax.shard_map(
        shards,
        mesh=mesh,
        in_specs=placed,
        out_specs=(P(both, None, None), P(None, "gx", "gy")),
        check_vma=False,
    )
```

```python
import functools

import jax
import jax.numpy as jnp
from jax import lax
from jax.experimental import pallas as pl
from jax.experimental.pallas import tpu as pltpu
from jax.sharding import PartitionSpec as P

BF = jnp.bfloat16
F32 = jnp.float32
GRANT = pltpu.CompilerParams(vmem_limit_bytes=20 * 1024 * 1024)
ANY = pl.BlockSpec(memory_space=pl.ANY)
VMEM = pl.BlockSpec(memory_space=pltpu.VMEM)


def dot(a, b, dims=((1,), (0,))):
    return lax.dot_general(a, b, (dims, ((), ())), preferred_element_type=F32)


def iota(shape, axis):
    return lax.broadcasted_iota(jnp.int32, shape, axis)


def prep_kernel(devices, capacity, ap_ref, bi_ref, am_ref, msg_ref, place_ref):
    tiles, traces = ap_ref.shape
    slots = devices * capacity
    width = am_ref.shape[2]
    depth = bi_ref.shape[1]
    before = (iota((traces, traces), 0) < iota((traces, traces), 1)).astype(BF)
    base = jnp.zeros((devices, 1), F32)
    amp = jnp.zeros((slots, width), F32)
    marks = jnp.zeros((slots, width), F32)
    for k in range(tiles):
        dest = ap_ref[k : k + 1, :]
        hit = iota((devices, traces), 0) == dest
        hits = hit.astype(F32)
        rank = jnp.sum(hits * (base + dot(hits.astype(BF), before)), axis=0, keepdims=True)
        base = base + jnp.sum(hits, axis=1, keepdims=True)
        pos = dest * capacity + rank.astype(jnp.int32)
        place = (iota((slots, traces), 0) == pos).astype(F32).astype(BF)
        place_ref[:, k * traces : (k + 1) * traces] = place
        amp = amp + dot(place, am_ref[:, k, :])
        levels = jnp.concatenate(
            [bi_ref[k].astype(F32), jnp.zeros((width - depth, traces), F32)], axis=0
        ).astype(BF)
        marks = marks + dot(place, levels, ((1,), (1,)))
    msg_ref[:, :width] = amp.astype(BF)
    msg_ref[:, width:] = marks.astype(BF)


def marks_kernel(msg_ref, tab_hbm, amp_ref, tab_ref, sem):
    width = amp_ref.shape[0]
    copy = pltpu.make_async_copy(tab_hbm, tab_ref, sem)
    copy.start()
    amp_ref[...] = msg_ref[:, :width].astype(F32).T.astype(BF)
    copy.wait()


def codes_kernel(blocks, place_ref, tt_ref, take_ref, pick_ref, drop_ref):
    tiles, depth, traces = tt_ref.shape
    group = 256 // blocks
    take_ref[...] = place_ref[...].astype(F32).T.astype(BF)
    size = depth * group
    lanes = 128
    at = iota((size, lanes), 1).astype(F32).astype(BF)
    row = iota((size, 1), 0)
    level = (row // group == iota((size, depth), 1)).astype(F32).astype(BF)
    for k in range(tiles):
        times = dot(level, tt_ref[k].astype(F32).astype(BF))
        for h in range(traces // group):
            own = iota((size, traces), 1) == row % group + h * group
            code = jnp.where(own, times, 0.0).astype(BF)
            code = dot(code, jnp.ones((traces, lanes), F32).astype(BF))
            code = (code + (row % group * blocks).astype(F32)).astype(BF)
            one, zero = jnp.ones_like(code), jnp.zeros_like(code)
            pick = jnp.concatenate(
                [jnp.where(code == at + BF(i), one, zero) for i in range(0, group * blocks, lanes)],
                axis=1,
            )
            pick_ref[k * (traces // group) + h] = pick
            drop_ref[k * (traces // group) + h] = pick.astype(F32).T.astype(BF)


def by_band(band, values, bands):
    zero = jnp.zeros_like(values)
    return jnp.concatenate([jnp.where(band == BF(b), values, zero) for b in range(bands)], axis=1)


def put(ref, z, value):
    if len(ref.shape) == 4:
        ref[:, z] = value.reshape(ref.shape[0], ref.shape[2], ref.shape[3])
    else:
        ref[z] = value


def get(ref, z):
    if len(ref.shape) == 4:
        return ref[:, z].reshape(ref.shape[0] * ref.shape[2], ref.shape[3])
    return ref[z]


def rows_kernel(
    per,
    cols,
    image_hbm,
    tab_hbm,
    out_hbm,
    image_ref,
    tab_ref,
    turn_ref,
    out_ref,
    image_sem,
    tab_sem,
    out_sem,
):
    depth, width, cells = image_ref.shape
    pieces, strips = depth // per, tab_ref.shape[0] // cols

    def image_copy(m):
        at = pl.ds(m * per, per)
        return pltpu.make_async_copy(image_hbm.at[at], image_ref.at[at], image_sem.at[m])

    def tab_copy(n):
        at = pl.ds(n * cols, cols)
        return pltpu.make_async_copy(tab_hbm.at[at], tab_ref.at[at], tab_sem.at[n])

    tab_copy(0).start()
    for m in range(pieces):
        image_copy(m).start()
    for n in range(1, strips):
        tab_copy(n).start()
    sent = []
    tab_copy(0).wait()
    turn_ref[0] = tab_ref[:cols, :].T
    for n in range(strips):
        for m in range(pieces):
            if n == 0:
                image_copy(m).wait()
            if m == pieces - 1 and n + 1 < strips:
                tab_copy(n + 1).wait()
                turn_ref[n + 1] = tab_ref[(n + 1) * cols : (n + 2) * cols, :].T
            levels = image_ref[m * per : (m + 1) * per].reshape(per * width, cells)
            rows = dot(levels, turn_ref[n]).astype(BF)
            out_ref[m * per : (m + 1) * per, :, n * cols : (n + 1) * cols] = rows.reshape(
                per, width, cols
            )
            at = (pl.ds(m * per, per), slice(None), pl.ds(n * cols, cols))
            copy = pltpu.make_async_copy(
                out_ref.at[at], out_hbm.at[at], out_sem.at[n * pieces + m]
            )
            copy.start()
            sent.append(copy)
    for copy in sent:
        copy.wait()


def demig_kernel(bands, per, msg_ref, rows_hbm, out_ref, rows_ref, sem):
    depth, width, long = rows_ref.shape
    block_len = long // bands
    pieces = depth // per

    def rows_copy(m):
        at = pl.ds(m * per, per)
        return pltpu.make_async_copy(rows_hbm.at[at], rows_ref.at[at], sem.at[m])

    for m in range(pieces):
        rows_copy(m).start()
    amp = msg_ref[:, :width]
    marks = msg_ref[:, width:].astype(F32)
    for m in range(pieces):
        rows_copy(m).wait()
        for z in range(m * per, (m + 1) * per):
            band = jnp.broadcast_to(marks[:, z : z + 1], amp.shape).astype(BF)
            rows = jnp.concatenate(
                [rows_ref[z, :, b * block_len : (b + 1) * block_len] for b in range(bands)], axis=0
            )
            put(out_ref, z, dot(by_band(band, amp, bands), rows).astype(BF))


def residual_kernel(
    place_ref, take_ref, pick_ref, drop_ref, obs_ref, recv_ref, res_ref, send_ref, pair_ref
):
    depth = pair_ref.shape[0]
    traces, blocks, block_len = obs_ref.shape
    group = 256 // blocks
    halves = traces // group
    tiles = pick_ref.shape[0] // halves
    take = take_ref[...]
    for z in range(0, depth, 2):
        two = dot(take, jnp.concatenate([get(recv_ref, z), get(recv_ref, z + 1)], axis=1)).astype(BF)
        pair_ref[z] = two[:, :block_len]
        pair_ref[z + 1] = two[:, block_len:]
    for h in range(halves):
        total = -obs_ref[h * group : (h + 1) * group].astype(F32).reshape(group * blocks, block_len)
        for k in range(tiles):
            at = slice(k * traces + h * group, k * traces + (h + 1) * group)
            part = pair_ref[:, at, :].reshape(depth * group, block_len)
            total = total + dot(drop_ref[k * halves + h], part)
        res_ref[h * group : (h + 1) * group] = total.reshape(group, blocks, block_len)
        low = total.astype(BF)
        for k in range(tiles):
            at = slice(k * traces + h * group, k * traces + (h + 1) * group)
            got = dot(pick_ref[k * halves + h], low).astype(BF)
            pair_ref[:, at, :] = got.reshape(depth, group, block_len)
    place = place_ref[...]
    for z in range(0, depth, 2):
        two = dot(place, jnp.concatenate([pair_ref[z], pair_ref[z + 1]], axis=1)).astype(BF)
        put(send_ref, z, two[:, :block_len])
        put(send_ref, z + 1, two[:, block_len:])


def image_kernel(
    bands, per, msg_ref, amp_ref, blk_ref, tab_ref, out_hbm, stack_ref, out_ref, sem
):
    depth, width, cells = out_ref.shape
    marks = msg_ref[:, width:].astype(F32)
    sent = []
    for m in range(depth // per):
        for z in range(m * per, (m + 1) * per):
            picked = get(blk_ref, z)
            band = jnp.broadcast_to(marks[:, z : z + 1], picked.shape).astype(BF)
            masked = by_band(band, picked, bands)
            stack_ref[z * width : (z + 1) * width, :] = dot(amp_ref[...], masked).astype(BF)
        stack = stack_ref[m * per * width : (m + 1) * per * width, :]
        out_ref[m * per : (m + 1) * per] = dot(stack, tab_ref[...]).reshape(per, width, cells)
        at = pl.ds(m * per, per)
        copy = pltpu.make_async_copy(out_ref.at[at], out_hbm.at[at], sem.at[m])
        copy.start()
        sent.append(copy)
    for copy in sent:
        copy.wait()


def shards(model_image, tables, observed, aperture, traveltime, band_index, amplitude):
    devices = lax.axis_size("gx") * lax.axis_size("gy")
    depth, width_x, width_y = model_image.shape
    bands, block_len, _ = tables.shape
    traces, tile_count = aperture.shape
    blocks = observed.shape[1]
    capacity = max(2, 2 * traces * tile_count // devices)
    slots = devices * capacity
    pairs = traces * tile_count
    long = bands * block_len
    aligned = capacity % 8 == 0
    groups = pairs * blocks // 256
    tables_flat = tables.reshape(long, width_y)

    def cost(flops, moved):
        return pl.CostEstimate(flops=flops, bytes_accessed=moved, transcendentals=0)

    def shape_of(count):
        if aligned:
            return (devices, count, capacity, block_len)
        return (count, slots, block_len)

    def exchange(x):
        if not aligned:
            x = x.reshape(-1, devices, capacity, block_len).transpose(1, 0, 2, 3)
        x = lax.all_to_all(x, ("gx", "gy"), split_axis=0, concat_axis=0, tiled=True)
        if not aligned:
            x = x.transpose(1, 0, 2, 3).reshape(-1, slots, block_len)
        return x

    message, place = pl.pallas_call(
        functools.partial(prep_kernel, devices, capacity),
        out_shape=(
            jax.ShapeDtypeStruct((slots, 2 * width_x), BF),
            jax.ShapeDtypeStruct((slots, pairs), BF),
        ),
        in_specs=[VMEM] * 3,
        out_specs=(VMEM, VMEM),
        name="prep",
    )(aperture.T, band_index.transpose(1, 2, 0), amplitude)
    got = lax.all_to_all(message, ("gx", "gy"), split_axis=0, concat_axis=0, tiled=True)

    per, cols = depth // 2, long // 2
    rows = pl.pallas_call(
        functools.partial(rows_kernel, per, cols),
        out_shape=jax.ShapeDtypeStruct((depth, width_x, long), BF),
        in_specs=[ANY, ANY],
        out_specs=ANY,
        scratch_shapes=[
            pltpu.VMEM((depth, width_x, width_y), BF),
            pltpu.VMEM((long, width_y), BF),
            pltpu.VMEM((long // cols, width_y, cols), BF),
            pltpu.VMEM((depth, width_x, long), BF),
            pltpu.SemaphoreType.DMA((depth // per,)),
            pltpu.SemaphoreType.DMA((long // cols,)),
            pltpu.SemaphoreType.DMA((depth // per * (long // cols),)),
        ],
        cost_estimate=cost(2 * depth * width_x * width_y * long, 4 * depth * width_x * width_y),
        name="rows",
    )(model_image, tables_flat)
    rows = pltpu.with_memory_space_constraint(rows, pltpu.HBM)
    per = 4
    partials = pl.pallas_call(
        functools.partial(demig_kernel, bands, per),
        out_shape=jax.ShapeDtypeStruct(shape_of(depth), BF),
        in_specs=[VMEM, ANY],
        out_specs=VMEM,
        scratch_shapes=[
            pltpu.VMEM((depth, width_x, long), BF),
            pltpu.SemaphoreType.DMA((depth // per,)),
        ],
        compiler_params=GRANT,
        cost_estimate=cost(2 * depth * slots * width_x * long, 2 * depth * width_x * long),
        name="demig",
    )(got, rows)
    returned = exchange(partials)
    take, pick, drop = pl.pallas_call(
        functools.partial(codes_kernel, blocks),
        out_shape=(
            jax.ShapeDtypeStruct((pairs, slots), BF),
            jax.ShapeDtypeStruct((groups, 256, 256), BF),
            jax.ShapeDtypeStruct((groups, 256, 256), BF),
        ),
        in_specs=[VMEM] * 2,
        out_specs=(VMEM,) * 3,
        compiler_params=GRANT,
        cost_estimate=cost(groups * 256 * 256 * 256, groups * 256 * 256 * 4),
        name="codes",
    )(place, traveltime.transpose(1, 2, 0))
    residual, outgoing = pl.pallas_call(
        residual_kernel,
        out_shape=(
            jax.ShapeDtypeStruct((traces, blocks, block_len), F32),
            jax.ShapeDtypeStruct(shape_of(depth), BF),
        ),
        in_specs=[VMEM] * 6,
        out_specs=(VMEM, VMEM),
        scratch_shapes=[pltpu.VMEM((depth, pairs, block_len), BF)],
        compiler_params=GRANT,
        cost_estimate=cost(4 * depth * slots * pairs * block_len, 4 * depth * slots * block_len),
        name="resid",
    )(place, take, pick, drop, observed, returned)
    incoming = exchange(outgoing)
    _, got_late = lax.optimization_barrier((residual, got))
    turned, tables_near = pl.pallas_call(
        marks_kernel,
        out_shape=(
            jax.ShapeDtypeStruct((width_x, slots), BF),
            jax.ShapeDtypeStruct((long, width_y), BF),
        ),
        in_specs=[VMEM, ANY],
        out_specs=(VMEM,) * 2,
        scratch_shapes=[pltpu.SemaphoreType.DMA],
        compiler_params=GRANT,
        cost_estimate=cost(slots * width_x, 4 * long * width_y),
        name="marks",
    )(got_late, pltpu.with_memory_space_constraint(tables_flat, pltpu.HBM))
    per = 2
    gradient = pl.pallas_call(
        functools.partial(image_kernel, bands, per),
        out_shape=jax.ShapeDtypeStruct((depth, width_x, width_y), F32),
        in_specs=[VMEM] * 4,
        out_specs=ANY,
        scratch_shapes=[
            pltpu.VMEM((depth * width_x, long), BF),
            pltpu.VMEM((depth, width_x, width_y), F32),
            pltpu.SemaphoreType.DMA((depth // per,)),
        ],
        compiler_params=pltpu.CompilerParams(vmem_limit_bytes=32 * 1024 * 1024),
        cost_estimate=cost(
            2 * depth * width_x * long * (width_y + slots), 4 * depth * width_x * width_y
        ),
        name="image",
    )(got, turned, incoming, tables_near)
    return residual, gradient


def solution(mesh):
    both = ("gx", "gy")
    placed = (
        P(None, "gx", "gy"),
        P(),
        P(both, None, None),
        P(both, None),
        P(both, None, None),
        P(both, None, None),
        P(both, None, None),
    )
    return jax.shard_map(
        shards,
        mesh=mesh,
        in_specs=placed,
        out_specs=(P(both, None, None), P(None, "gx", "gy")),
        check_vma=False,
    )
```

```python
import functools

import jax
import jax.numpy as jnp
from jax import lax
from jax.experimental import pallas as pl
from jax.experimental.pallas import tpu as pltpu
from jax.sharding import PartitionSpec as P

BF = jnp.bfloat16
F32 = jnp.float32
GRANT = pltpu.CompilerParams(vmem_limit_bytes=20 * 1024 * 1024)
ANY = pl.BlockSpec(memory_space=pl.ANY)
VMEM = pl.BlockSpec(memory_space=pltpu.VMEM)


def dot(a, b, dims=((1,), (0,))):
    return lax.dot_general(a, b, (dims, ((), ())), preferred_element_type=F32)


def iota(shape, axis):
    return lax.broadcasted_iota(jnp.int32, shape, axis)


def prep_kernel(devices, capacity, ap_ref, bi_ref, am_ref, msg_ref, place_ref):
    tiles, traces = ap_ref.shape
    slots = devices * capacity
    width = am_ref.shape[2]
    depth = bi_ref.shape[1]
    before = (iota((traces, traces), 0) < iota((traces, traces), 1)).astype(BF)
    base = jnp.zeros((devices, 1), F32)
    amp = jnp.zeros((slots, width), F32)
    marks = jnp.zeros((slots, width), F32)
    for k in range(tiles):
        dest = ap_ref[k : k + 1, :]
        hit = iota((devices, traces), 0) == dest
        hits = hit.astype(F32)
        rank = jnp.sum(hits * (base + dot(hits.astype(BF), before)), axis=0, keepdims=True)
        base = base + jnp.sum(hits, axis=1, keepdims=True)
        pos = dest * capacity + rank.astype(jnp.int32)
        place = (iota((slots, traces), 0) == pos).astype(F32).astype(BF)
        place_ref[:, k * traces : (k + 1) * traces] = place
        amp = amp + dot(place, am_ref[:, k, :])
        levels = jnp.concatenate(
            [bi_ref[k].astype(F32), jnp.zeros((width - depth, traces), F32)], axis=0
        ).astype(BF)
        marks = marks + dot(place, levels, ((1,), (1,)))
    msg_ref[:, :width] = amp.astype(BF)
    msg_ref[:, width:] = marks.astype(BF)


def codes_kernel(blocks, msg_ref, place_ref, tt_ref, take_ref, pick_ref, drop_ref, amp_ref):
    tiles, depth, traces = tt_ref.shape
    group = 256 // blocks
    width = amp_ref.shape[0]
    amp_ref[...] = msg_ref[:, :width].astype(F32).T.astype(BF)
    take_ref[...] = place_ref[...].astype(F32).T.astype(BF)
    size = depth * group
    lanes = 128
    at = iota((size, lanes), 1).astype(F32).astype(BF)
    row = iota((size, 1), 0)
    level = (row // group == iota((size, depth), 1)).astype(F32).astype(BF)
    for k in range(tiles):
        times = dot(level, tt_ref[k].astype(F32).astype(BF))
        for h in range(traces // group):
            own = iota((size, traces), 1) == row % group + h * group
            code = jnp.where(own, times, 0.0).astype(BF)
            code = dot(code, jnp.ones((traces, lanes), F32).astype(BF))
            code = (code + (row % group * blocks).astype(F32)).astype(BF)
            one, zero = jnp.ones_like(code), jnp.zeros_like(code)
            pick = jnp.concatenate(
                [jnp.where(code == at + BF(i), one, zero) for i in range(0, group * blocks, lanes)],
                axis=1,
            )
            pick_ref[k * (traces // group) + h] = pick
            drop_ref[k * (traces // group) + h] = pick.astype(F32).T.astype(BF)


def by_band(band, values, bands):
    zero = jnp.zeros_like(values)
    return jnp.concatenate([jnp.where(band == BF(b), values, zero) for b in range(bands)], axis=1)


def put(ref, z, value):
    if len(ref.shape) == 4:
        ref[:, z] = value.reshape(ref.shape[0], ref.shape[2], ref.shape[3])
    else:
        ref[z] = value


def get(ref, z):
    if len(ref.shape) == 4:
        return ref[:, z].reshape(ref.shape[0] * ref.shape[2], ref.shape[3])
    return ref[z]


def rows_kernel(
    per,
    cols,
    image_hbm,
    tab_hbm,
    out_hbm,
    image_ref,
    tab_ref,
    turn_ref,
    out_ref,
    image_sem,
    tab_sem,
    out_sem,
):
    depth, width, cells = image_ref.shape
    pieces, strips = depth // per, tab_ref.shape[0] // cols

    def image_copy(m):
        at = pl.ds(m * per, per)
        return pltpu.make_async_copy(image_hbm.at[at], image_ref.at[at], image_sem.at[m])

    def tab_copy(n):
        at = pl.ds(n * cols, cols)
        return pltpu.make_async_copy(tab_hbm.at[at], tab_ref.at[at], tab_sem.at[n])

    tab_copy(0).start()
    for m in range(pieces):
        image_copy(m).start()
    for n in range(1, strips):
        tab_copy(n).start()
    sent = []
    tab_copy(0).wait()
    turn_ref[0] = tab_ref[:cols, :].T
    for n in range(strips):
        for m in range(pieces):
            if n == 0:
                image_copy(m).wait()
            if m == pieces - 1 and n + 1 < strips:
                tab_copy(n + 1).wait()
                turn_ref[n + 1] = tab_ref[(n + 1) * cols : (n + 2) * cols, :].T
            levels = image_ref[m * per : (m + 1) * per].reshape(per * width, cells)
            rows = dot(levels, turn_ref[n]).astype(BF)
            out_ref[m * per : (m + 1) * per, :, n * cols : (n + 1) * cols] = rows.reshape(
                per, width, cols
            )
            at = (pl.ds(m * per, per), slice(None), pl.ds(n * cols, cols))
            copy = pltpu.make_async_copy(
                out_ref.at[at], out_hbm.at[at], out_sem.at[n * pieces + m]
            )
            copy.start()
            sent.append(copy)
    for copy in sent:
        copy.wait()


def demig_kernel(bands, per, msg_ref, rows_hbm, out_ref, rows_ref, sem):
    depth, width, long = rows_ref.shape
    block_len = long // bands
    pieces = depth // per

    def rows_copy(m):
        at = pl.ds(m * per, per)
        return pltpu.make_async_copy(rows_hbm.at[at], rows_ref.at[at], sem.at[m])

    for m in range(pieces):
        rows_copy(m).start()
    amp = msg_ref[:, :width]
    marks = msg_ref[:, width:].astype(F32)
    for m in range(pieces):
        rows_copy(m).wait()
        for z in range(m * per, (m + 1) * per):
            band = jnp.broadcast_to(marks[:, z : z + 1], amp.shape).astype(BF)
            rows = jnp.concatenate(
                [rows_ref[z, :, b * block_len : (b + 1) * block_len] for b in range(bands)], axis=0
            )
            put(out_ref, z, dot(by_band(band, amp, bands), rows).astype(BF))


def residual_kernel(
    place_ref, take_ref, pick_ref, drop_ref, obs_ref, recv_ref, res_ref, send_ref, pair_ref
):
    depth = pair_ref.shape[0]
    traces, blocks, block_len = obs_ref.shape
    group = 256 // blocks
    halves = traces // group
    tiles = pick_ref.shape[0] // halves
    take = take_ref[...]
    for z in range(0, depth, 2):
        two = dot(take, jnp.concatenate([get(recv_ref, z), get(recv_ref, z + 1)], axis=1)).astype(BF)
        pair_ref[z] = two[:, :block_len]
        pair_ref[z + 1] = two[:, block_len:]
    for h in range(halves):
        total = -obs_ref[h * group : (h + 1) * group].astype(F32).reshape(group * blocks, block_len)
        for k in range(tiles):
            at = slice(k * traces + h * group, k * traces + (h + 1) * group)
            part = pair_ref[:, at, :].reshape(depth * group, block_len)
            total = total + dot(drop_ref[k * halves + h], part)
        res_ref[h * group : (h + 1) * group] = total.reshape(group, blocks, block_len)
        low = total.astype(BF)
        for k in range(tiles):
            at = slice(k * traces + h * group, k * traces + (h + 1) * group)
            got = dot(pick_ref[k * halves + h], low).astype(BF)
            pair_ref[:, at, :] = got.reshape(depth, group, block_len)
    place = place_ref[...]
    for z in range(0, depth, 2):
        two = dot(place, jnp.concatenate([pair_ref[z], pair_ref[z + 1]], axis=1)).astype(BF)
        put(send_ref, z, two[:, :block_len])
        put(send_ref, z + 1, two[:, block_len:])


def image_kernel(
    bands, per, msg_ref, amp_ref, blk_ref, tab_ref, out_hbm, stack_ref, out_ref, sem
):
    depth, width, cells = out_ref.shape
    marks = msg_ref[:, width:].astype(F32)
    sent = []
    for m in range(depth // per):
        for z in range(m * per, (m + 1) * per):
            picked = get(blk_ref, z)
            band = jnp.broadcast_to(marks[:, z : z + 1], picked.shape).astype(BF)
            masked = by_band(band, picked, bands)
            stack_ref[z * width : (z + 1) * width, :] = dot(amp_ref[...], masked).astype(BF)
        stack = stack_ref[m * per * width : (m + 1) * per * width, :]
        out_ref[m * per : (m + 1) * per] = dot(stack, tab_ref[...]).reshape(per, width, cells)
        at = pl.ds(m * per, per)
        copy = pltpu.make_async_copy(out_ref.at[at], out_hbm.at[at], sem.at[m])
        copy.start()
        sent.append(copy)
    for copy in sent:
        copy.wait()


def shards(model_image, tables, observed, aperture, traveltime, band_index, amplitude):
    devices = lax.axis_size("gx") * lax.axis_size("gy")
    depth, width_x, width_y = model_image.shape
    bands, block_len, _ = tables.shape
    traces, tile_count = aperture.shape
    blocks = observed.shape[1]
    capacity = max(2, 2 * traces * tile_count // devices)
    slots = devices * capacity
    pairs = traces * tile_count
    long = bands * block_len
    aligned = capacity % 8 == 0
    groups = pairs * blocks // 256
    tables_flat = tables.reshape(long, width_y)

    def cost(flops, moved):
        return pl.CostEstimate(flops=flops, bytes_accessed=moved, transcendentals=0)

    def shape_of(count):
        if aligned:
            return (devices, count, capacity, block_len)
        return (count, slots, block_len)

    def exchange(x):
        if not aligned:
            x = x.reshape(-1, devices, capacity, block_len).transpose(1, 0, 2, 3)
        x = lax.all_to_all(x, ("gx", "gy"), split_axis=0, concat_axis=0, tiled=True)
        if not aligned:
            x = x.transpose(1, 0, 2, 3).reshape(-1, slots, block_len)
        return x

    message, place = pl.pallas_call(
        functools.partial(prep_kernel, devices, capacity),
        out_shape=(
            jax.ShapeDtypeStruct((slots, 2 * width_x), BF),
            jax.ShapeDtypeStruct((slots, pairs), BF),
        ),
        in_specs=[VMEM] * 3,
        out_specs=(VMEM, VMEM),
        name="prep",
    )(aperture.T, band_index.transpose(1, 2, 0), amplitude)
    got = lax.all_to_all(message, ("gx", "gy"), split_axis=0, concat_axis=0, tiled=True)

    per, cols = depth // 2, long // 2
    rows = pl.pallas_call(
        functools.partial(rows_kernel, per, cols),
        out_shape=jax.ShapeDtypeStruct((depth, width_x, long), BF),
        in_specs=[ANY, ANY],
        out_specs=ANY,
        scratch_shapes=[
            pltpu.VMEM((depth, width_x, width_y), BF),
            pltpu.VMEM((long, width_y), BF),
            pltpu.VMEM((long // cols, width_y, cols), BF),
            pltpu.VMEM((depth, width_x, long), BF),
            pltpu.SemaphoreType.DMA((depth // per,)),
            pltpu.SemaphoreType.DMA((long // cols,)),
            pltpu.SemaphoreType.DMA((depth // per * (long // cols),)),
        ],
        cost_estimate=cost(2 * depth * width_x * width_y * long, 4 * depth * width_x * width_y),
        name="rows",
    )(model_image, tables_flat)
    rows = pltpu.with_memory_space_constraint(rows, pltpu.HBM)
    per = 4
    partials = pl.pallas_call(
        functools.partial(demig_kernel, bands, per),
        out_shape=jax.ShapeDtypeStruct(shape_of(depth), BF),
        in_specs=[VMEM, ANY],
        out_specs=VMEM,
        scratch_shapes=[
            pltpu.VMEM((depth, width_x, long), BF),
            pltpu.SemaphoreType.DMA((depth // per,)),
        ],
        compiler_params=GRANT,
        cost_estimate=cost(2 * depth * slots * width_x * long, 2 * depth * width_x * long),
        name="demig",
    )(got, rows)
    returned = exchange(partials)
    take, pick, drop, turned = pl.pallas_call(
        functools.partial(codes_kernel, blocks),
        out_shape=(
            jax.ShapeDtypeStruct((pairs, slots), BF),
            jax.ShapeDtypeStruct((groups, 256, 256), BF),
            jax.ShapeDtypeStruct((groups, 256, 256), BF),
            jax.ShapeDtypeStruct((width_x, slots), BF),
        ),
        in_specs=[VMEM] * 3,
        out_specs=(VMEM,) * 4,
        compiler_params=GRANT,
        cost_estimate=cost(groups * 256 * 256 * 256, groups * 256 * 256 * 4),
        name="codes",
    )(got, place, traveltime.transpose(1, 2, 0))
    residual, outgoing = pl.pallas_call(
        residual_kernel,
        out_shape=(
            jax.ShapeDtypeStruct((traces, blocks, block_len), F32),
            jax.ShapeDtypeStruct(shape_of(depth), BF),
        ),
        in_specs=[VMEM] * 6,
        out_specs=(VMEM, VMEM),
        scratch_shapes=[pltpu.VMEM((depth, pairs, block_len), BF)],
        compiler_params=GRANT,
        cost_estimate=cost(4 * depth * slots * pairs * block_len, 4 * depth * slots * block_len),
        name="resid",
    )(place, take, pick, drop, observed, returned)
    incoming = exchange(outgoing)
    per = 2
    gradient = pl.pallas_call(
        functools.partial(image_kernel, bands, per),
        out_shape=jax.ShapeDtypeStruct((depth, width_x, width_y), F32),
        in_specs=[VMEM] * 4,
        out_specs=ANY,
        scratch_shapes=[
            pltpu.VMEM((depth * width_x, long), BF),
            pltpu.VMEM((depth, width_x, width_y), F32),
            pltpu.SemaphoreType.DMA((depth // per,)),
        ],
        compiler_params=pltpu.CompilerParams(vmem_limit_bytes=32 * 1024 * 1024),
        cost_estimate=cost(
            2 * depth * width_x * long * (width_y + slots), 4 * depth * width_x * width_y
        ),
        name="image",
    )(got, turned, incoming, tables_flat)
    return residual, gradient


def solution(mesh):
    both = ("gx", "gy")
    placed = (
        P(None, "gx", "gy"),
        P(),
        P(both, None, None),
        P(both, None),
        P(both, None, None),
        P(both, None, None),
        P(both, None, None),
    )
    return jax.shard_map(
        shards,
        mesh=mesh,
        in_specs=placed,
        out_specs=(P(both, None, None), P(None, "gx", "gy")),
        check_vma=False,
    )
```

```python
import functools

import jax
import jax.numpy as jnp
from jax import lax
from jax.experimental import pallas as pl
from jax.experimental.pallas import tpu as pltpu
from jax.sharding import PartitionSpec as P

BF = jnp.bfloat16
F32 = jnp.float32
GRANT = pltpu.CompilerParams(vmem_limit_bytes=20 * 1024 * 1024)
ANY = pl.BlockSpec(memory_space=pl.ANY)
VMEM = pl.BlockSpec(memory_space=pltpu.VMEM)


def dot(a, b, dims=((1,), (0,))):
    return lax.dot_general(a, b, (dims, ((), ())), preferred_element_type=F32)


def iota(shape, axis):
    return lax.broadcasted_iota(jnp.int32, shape, axis)


def prep_kernel(devices, capacity, ap_ref, bi_ref, am_ref, msg_ref, place_ref):
    tiles, traces = ap_ref.shape
    slots = devices * capacity
    width = am_ref.shape[2]
    depth = bi_ref.shape[1]
    before = (iota((traces, traces), 0) < iota((traces, traces), 1)).astype(BF)
    base = jnp.zeros((devices, 1), F32)
    amp = jnp.zeros((slots, width), F32)
    marks = jnp.zeros((slots, width), F32)
    for k in range(tiles):
        dest = ap_ref[k : k + 1, :]
        hit = iota((devices, traces), 0) == dest
        hits = hit.astype(F32)
        rank = jnp.sum(hits * (base + dot(hits.astype(BF), before)), axis=0, keepdims=True)
        base = base + jnp.sum(hits, axis=1, keepdims=True)
        pos = dest * capacity + rank.astype(jnp.int32)
        place = (iota((slots, traces), 0) == pos).astype(F32).astype(BF)
        place_ref[:, k * traces : (k + 1) * traces] = place
        amp = amp + dot(place, am_ref[:, k, :])
        levels = jnp.concatenate(
            [bi_ref[k].astype(F32), jnp.zeros((width - depth, traces), F32)], axis=0
        ).astype(BF)
        marks = marks + dot(place, levels, ((1,), (1,)))
    msg_ref[:, :width] = amp.astype(BF)
    msg_ref[:, width:] = marks.astype(BF)


def fill_picks(blocks, tt_ref, pick_ref):
    tiles, depth, traces = tt_ref.shape
    group = 256 // blocks
    size = depth * group
    lanes = 128
    at = iota((size, lanes), 1).astype(F32).astype(BF)
    row = iota((size, 1), 0)
    level = (row // group == iota((size, depth), 1)).astype(F32).astype(BF)
    for k in range(tiles):
        times = dot(level, tt_ref[k].astype(F32).astype(BF))
        for h in range(traces // group):
            own = iota((size, traces), 1) == row % group + h * group
            code = jnp.where(own, times, 0.0).astype(BF)
            code = dot(code, jnp.ones((traces, lanes), F32).astype(BF))
            code = (code + (row % group * blocks).astype(F32)).astype(BF)
            one, zero = jnp.ones_like(code), jnp.zeros_like(code)
            pick_ref[k * (traces // group) + h] = jnp.concatenate(
                [jnp.where(code == at + BF(i), one, zero) for i in range(0, group * blocks, lanes)],
                axis=1,
            )


def by_band(band, values, bands):
    zero = jnp.zeros_like(values)
    return jnp.concatenate([jnp.where(band == BF(b), values, zero) for b in range(bands)], axis=1)


def put(ref, z, value):
    if len(ref.shape) == 4:
        ref[:, z] = value.reshape(ref.shape[0], ref.shape[2], ref.shape[3])
    else:
        ref[z] = value


def get(ref, z):
    if len(ref.shape) == 4:
        return ref[:, z].reshape(ref.shape[0] * ref.shape[2], ref.shape[3])
    return ref[z]


def rows_kernel(
    per,
    cols,
    image_hbm,
    tab_hbm,
    out_hbm,
    image_ref,
    tab_ref,
    turn_ref,
    out_ref,
    image_sem,
    tab_sem,
    out_sem,
):
    depth, width, cells = image_ref.shape
    pieces, strips = depth // per, tab_ref.shape[0] // cols

    def image_copy(m):
        at = pl.ds(m * per, per)
        return pltpu.make_async_copy(image_hbm.at[at], image_ref.at[at], image_sem.at[m])

    def tab_copy(n):
        at = pl.ds(n * cols, cols)
        return pltpu.make_async_copy(tab_hbm.at[at], tab_ref.at[at], tab_sem.at[n])

    tab_copy(0).start()
    for m in range(pieces):
        image_copy(m).start()
    for n in range(1, strips):
        tab_copy(n).start()
    sent = []
    tab_copy(0).wait()
    turn_ref[0] = tab_ref[:cols, :].T
    for n in range(strips):
        for m in range(pieces):
            if n == 0:
                image_copy(m).wait()
            if m == pieces - 1 and n + 1 < strips:
                tab_copy(n + 1).wait()
                turn_ref[n + 1] = tab_ref[(n + 1) * cols : (n + 2) * cols, :].T
            levels = image_ref[m * per : (m + 1) * per].reshape(per * width, cells)
            rows = dot(levels, turn_ref[n]).astype(BF)
            out_ref[m * per : (m + 1) * per, :, n * cols : (n + 1) * cols] = rows.reshape(
                per, width, cols
            )
            at = (pl.ds(m * per, per), slice(None), pl.ds(n * cols, cols))
            copy = pltpu.make_async_copy(
                out_ref.at[at], out_hbm.at[at], out_sem.at[n * pieces + m]
            )
            copy.start()
            sent.append(copy)
    for copy in sent:
        copy.wait()


def demig_kernel(bands, per, msg_ref, rows_hbm, out_ref, rows_ref, sem):
    depth, width, long = rows_ref.shape
    block_len = long // bands
    pieces = depth // per

    def rows_copy(m):
        at = pl.ds(m * per, per)
        return pltpu.make_async_copy(rows_hbm.at[at], rows_ref.at[at], sem.at[m])

    for m in range(pieces):
        rows_copy(m).start()
    amp = msg_ref[:, :width]
    marks = msg_ref[:, width:].astype(F32)
    for m in range(pieces):
        rows_copy(m).wait()
        for z in range(m * per, (m + 1) * per):
            band = jnp.broadcast_to(marks[:, z : z + 1], amp.shape).astype(BF)
            rows = jnp.concatenate(
                [rows_ref[z, :, b * block_len : (b + 1) * block_len] for b in range(bands)], axis=0
            )
            put(out_ref, z, dot(by_band(band, amp, bands), rows).astype(BF))


def residual_kernel(
    place_ref, tt_ref, obs_ref, recv_ref, res_ref, send_ref, pair_ref, pick_ref
):
    depth = pair_ref.shape[0]
    traces, blocks, block_len = obs_ref.shape
    group = 256 // blocks
    halves = traces // group
    tiles = pick_ref.shape[0] // halves
    take = place_ref[...].astype(F32).T.astype(BF)
    fill_picks(blocks, tt_ref, pick_ref)
    for z in range(0, depth, 2):
        two = dot(take, jnp.concatenate([get(recv_ref, z), get(recv_ref, z + 1)], axis=1)).astype(BF)
        pair_ref[z] = two[:, :block_len]
        pair_ref[z + 1] = two[:, block_len:]
    for h in range(halves):
        total = -obs_ref[h * group : (h + 1) * group].astype(F32).reshape(group * blocks, block_len)
        for k in range(tiles):
            at = slice(k * traces + h * group, k * traces + (h + 1) * group)
            part = pair_ref[:, at, :].reshape(depth * group, block_len)
            total = total + dot(pick_ref[k * halves + h], part, ((0,), (0,)))
        res_ref[h * group : (h + 1) * group] = total.reshape(group, blocks, block_len)
        low = total.astype(BF)
        for k in range(tiles):
            at = slice(k * traces + h * group, k * traces + (h + 1) * group)
            got = dot(pick_ref[k * halves + h], low).astype(BF)
            pair_ref[:, at, :] = got.reshape(depth, group, block_len)
    place = place_ref[...]
    for z in range(0, depth, 2):
        two = dot(place, jnp.concatenate([pair_ref[z], pair_ref[z + 1]], axis=1)).astype(BF)
        put(send_ref, z, two[:, :block_len])
        put(send_ref, z + 1, two[:, block_len:])


def image_kernel(
    bands, per, msg_ref, blk_ref, tab_ref, out_hbm, stack_ref, out_ref, sem
):
    depth, width, cells = out_ref.shape
    amp = msg_ref[:, :width].astype(F32).T.astype(BF)
    marks = msg_ref[:, width:].astype(F32)
    sent = []
    for m in range(depth // per):
        for z in range(m * per, (m + 1) * per):
            picked = get(blk_ref, z)
            band = jnp.broadcast_to(marks[:, z : z + 1], picked.shape).astype(BF)
            masked = by_band(band, picked, bands)
            stack_ref[z * width : (z + 1) * width, :] = dot(amp, masked).astype(BF)
        stack = stack_ref[m * per * width : (m + 1) * per * width, :]
        out_ref[m * per : (m + 1) * per] = dot(stack, tab_ref[...]).reshape(per, width, cells)
        at = pl.ds(m * per, per)
        copy = pltpu.make_async_copy(out_ref.at[at], out_hbm.at[at], sem.at[m])
        copy.start()
        sent.append(copy)
    for copy in sent:
        copy.wait()


def shards(model_image, tables, observed, aperture, traveltime, band_index, amplitude):
    devices = lax.axis_size("gx") * lax.axis_size("gy")
    depth, width_x, width_y = model_image.shape
    bands, block_len, _ = tables.shape
    traces, tile_count = aperture.shape
    blocks = observed.shape[1]
    capacity = max(2, 2 * traces * tile_count // devices)
    slots = devices * capacity
    pairs = traces * tile_count
    long = bands * block_len
    aligned = capacity % 8 == 0
    groups = pairs * blocks // 256
    tables_flat = tables.reshape(long, width_y)

    def cost(flops, moved):
        return pl.CostEstimate(flops=flops, bytes_accessed=moved, transcendentals=0)

    def shape_of(count):
        if aligned:
            return (devices, count, capacity, block_len)
        return (count, slots, block_len)

    def exchange(x):
        if not aligned:
            x = x.reshape(-1, devices, capacity, block_len).transpose(1, 0, 2, 3)
        x = lax.all_to_all(x, ("gx", "gy"), split_axis=0, concat_axis=0, tiled=True)
        if not aligned:
            x = x.transpose(1, 0, 2, 3).reshape(-1, slots, block_len)
        return x

    message, place = pl.pallas_call(
        functools.partial(prep_kernel, devices, capacity),
        out_shape=(
            jax.ShapeDtypeStruct((slots, 2 * width_x), BF),
            jax.ShapeDtypeStruct((slots, pairs), BF),
        ),
        in_specs=[VMEM] * 3,
        out_specs=(VMEM, VMEM),
        name="prep",
    )(aperture.T, band_index.transpose(1, 2, 0), amplitude)
    got = lax.all_to_all(message, ("gx", "gy"), split_axis=0, concat_axis=0, tiled=True)

    per, cols = depth // 2, long // 2
    rows = pl.pallas_call(
        functools.partial(rows_kernel, per, cols),
        out_shape=jax.ShapeDtypeStruct((depth, width_x, long), BF),
        in_specs=[ANY, ANY],
        out_specs=ANY,
        scratch_shapes=[
            pltpu.VMEM((depth, width_x, width_y), BF),
            pltpu.VMEM((long, width_y), BF),
            pltpu.VMEM((long // cols, width_y, cols), BF),
            pltpu.VMEM((depth, width_x, long), BF),
            pltpu.SemaphoreType.DMA((depth // per,)),
            pltpu.SemaphoreType.DMA((long // cols,)),
            pltpu.SemaphoreType.DMA((depth // per * (long // cols),)),
        ],
        cost_estimate=cost(2 * depth * width_x * width_y * long, 4 * depth * width_x * width_y),
        name="rows",
    )(model_image, tables_flat)
    rows = pltpu.with_memory_space_constraint(rows, pltpu.HBM)
    per = 4
    partials = pl.pallas_call(
        functools.partial(demig_kernel, bands, per),
        out_shape=jax.ShapeDtypeStruct(shape_of(depth), BF),
        in_specs=[VMEM, ANY],
        out_specs=VMEM,
        scratch_shapes=[
            pltpu.VMEM((depth, width_x, long), BF),
            pltpu.SemaphoreType.DMA((depth // per,)),
        ],
        compiler_params=GRANT,
        cost_estimate=cost(2 * depth * slots * width_x * long, 2 * depth * width_x * long),
        name="demig",
    )(got, rows)
    returned = exchange(partials)
    residual, outgoing = pl.pallas_call(
        residual_kernel,
        out_shape=(
            jax.ShapeDtypeStruct((traces, blocks, block_len), F32),
            jax.ShapeDtypeStruct(shape_of(depth), BF),
        ),
        in_specs=[VMEM] * 4,
        out_specs=(VMEM, VMEM),
        scratch_shapes=[
            pltpu.VMEM((depth, pairs, block_len), BF),
            pltpu.VMEM((groups, 256, 256), BF),
        ],
        compiler_params=GRANT,
        cost_estimate=cost(4 * depth * slots * pairs * block_len, 4 * depth * slots * block_len),
        name="resid",
    )(place, traveltime.transpose(1, 2, 0), observed, returned)
    incoming = exchange(outgoing)
    per = 2
    gradient = pl.pallas_call(
        functools.partial(image_kernel, bands, per),
        out_shape=jax.ShapeDtypeStruct((depth, width_x, width_y), F32),
        in_specs=[VMEM] * 3,
        out_specs=ANY,
        scratch_shapes=[
            pltpu.VMEM((depth * width_x, long), BF),
            pltpu.VMEM((depth, width_x, width_y), F32),
            pltpu.SemaphoreType.DMA((depth // per,)),
        ],
        compiler_params=pltpu.CompilerParams(vmem_limit_bytes=32 * 1024 * 1024),
        cost_estimate=cost(
            2 * depth * width_x * long * (width_y + slots), 4 * depth * width_x * width_y
        ),
        name="image",
    )(got, incoming, tables_flat)
    return residual, gradient


def solution(mesh):
    both = ("gx", "gy")
    placed = (
        P(None, "gx", "gy"),
        P(),
        P(both, None, None),
        P(both, None),
        P(both, None, None),
        P(both, None, None),
        P(both, None, None),
    )
    return jax.shard_map(
        shards,
        mesh=mesh,
        in_specs=placed,
        out_specs=(P(both, None, None), P(None, "gx", "gy")),
        check_vma=False,
    )
```

```python
import functools

import jax
import jax.numpy as jnp
from jax import lax
from jax.experimental import pallas as pl
from jax.experimental.pallas import tpu as pltpu
from jax.sharding import PartitionSpec as P

BF = jnp.bfloat16
F32 = jnp.float32
GRANT = pltpu.CompilerParams(vmem_limit_bytes=20 * 1024 * 1024)
ANY = pl.BlockSpec(memory_space=pl.ANY)
VMEM = pl.BlockSpec(memory_space=pltpu.VMEM)


def dot(a, b, dims=((1,), (0,))):
    return lax.dot_general(a, b, (dims, ((), ())), preferred_element_type=F32)


def iota(shape, axis):
    return lax.broadcasted_iota(jnp.int32, shape, axis)


def prep_kernel(devices, capacity, ap_ref, bi_ref, am_ref, msg_ref, place_ref):
    tiles, traces = ap_ref.shape
    slots = devices * capacity
    width = am_ref.shape[2]
    depth = bi_ref.shape[1]
    before = (iota((traces, traces), 0) < iota((traces, traces), 1)).astype(BF)
    base = jnp.zeros((devices, 1), F32)
    amp = jnp.zeros((slots, width), F32)
    marks = jnp.zeros((slots, width), F32)
    for k in range(tiles):
        dest = ap_ref[k : k + 1, :]
        hit = iota((devices, traces), 0) == dest
        hits = hit.astype(F32)
        rank = jnp.sum(hits * (base + dot(hits.astype(BF), before)), axis=0, keepdims=True)
        base = base + jnp.sum(hits, axis=1, keepdims=True)
        pos = dest * capacity + rank.astype(jnp.int32)
        place = (iota((slots, traces), 0) == pos).astype(F32).astype(BF)
        place_ref[:, k * traces : (k + 1) * traces] = place
        amp = amp + dot(place, am_ref[:, k, :])
        levels = jnp.concatenate(
            [bi_ref[k].astype(F32), jnp.zeros((width - depth, traces), F32)], axis=0
        ).astype(BF)
        marks = marks + dot(place, levels, ((1,), (1,)))
    msg_ref[:, :width] = amp.astype(BF)
    msg_ref[:, width:] = marks.astype(BF)


def codes_kernel(blocks, msg_ref, place_ref, tt_ref, take_ref, pick_ref, drop_ref, amp_ref):
    tiles, depth, traces = tt_ref.shape
    group = 256 // blocks
    width = amp_ref.shape[0]
    amp_ref[...] = msg_ref[:, :width].astype(F32).T.astype(BF)
    take_ref[...] = place_ref[...].astype(F32).T.astype(BF)
    size = depth * group
    lanes = 128
    at = iota((size, lanes), 1).astype(F32).astype(BF)
    row = iota((size, 1), 0)
    level = (row // group == iota((size, depth), 1)).astype(F32).astype(BF)
    for k in range(tiles):
        times = dot(level, tt_ref[k].astype(F32).astype(BF))
        for h in range(traces // group):
            own = iota((size, traces), 1) == row % group + h * group
            code = jnp.where(own, times, 0.0).astype(BF)
            code = dot(code, jnp.ones((traces, lanes), F32).astype(BF))
            code = (code + (row % group * blocks).astype(F32)).astype(BF)
            one, zero = jnp.ones_like(code), jnp.zeros_like(code)
            pick = jnp.concatenate(
                [jnp.where(code == at + BF(i), one, zero) for i in range(0, group * blocks, lanes)],
                axis=1,
            )
            pick_ref[k * (traces // group) + h] = pick
            drop_ref[k * (traces // group) + h] = pick.astype(F32).T.astype(BF)


def by_band(band, values, bands):
    zero = jnp.zeros_like(values)
    return jnp.concatenate([jnp.where(band == BF(b), values, zero) for b in range(bands)], axis=1)


def put(ref, z, value):
    if len(ref.shape) == 4:
        ref[:, z] = value.reshape(ref.shape[0], ref.shape[2], ref.shape[3])
    else:
        ref[z] = value


def get(ref, z):
    if len(ref.shape) == 4:
        return ref[:, z].reshape(ref.shape[0] * ref.shape[2], ref.shape[3])
    return ref[z]


def rows_kernel(
    per,
    cols,
    image_hbm,
    tab_hbm,
    out_hbm,
    image_ref,
    tab_ref,
    turn_ref,
    out_ref,
    image_sem,
    tab_sem,
    out_sem,
):
    depth, width, cells = image_ref.shape
    pieces, strips = depth // per, tab_ref.shape[0] // cols

    def image_copy(m):
        at = pl.ds(m * per, per)
        return pltpu.make_async_copy(image_hbm.at[at], image_ref.at[at], image_sem.at[m])

    def tab_copy(n):
        at = pl.ds(n * cols, cols)
        return pltpu.make_async_copy(tab_hbm.at[at], tab_ref.at[at], tab_sem.at[n])

    tab_copy(0).start()
    for m in range(pieces):
        image_copy(m).start()
    for n in range(1, strips):
        tab_copy(n).start()
    sent = []
    tab_copy(0).wait()
    turn_ref[0] = tab_ref[:cols, :].T
    for n in range(strips):
        for m in range(pieces):
            if n == 0:
                image_copy(m).wait()
            if m == pieces - 1 and n + 1 < strips:
                tab_copy(n + 1).wait()
                turn_ref[n + 1] = tab_ref[(n + 1) * cols : (n + 2) * cols, :].T
            levels = image_ref[m * per : (m + 1) * per].reshape(per * width, cells)
            rows = dot(levels, turn_ref[n]).astype(BF)
            out_ref[m * per : (m + 1) * per, :, n * cols : (n + 1) * cols] = rows.reshape(
                per, width, cols
            )
            at = (pl.ds(m * per, per), slice(None), pl.ds(n * cols, cols))
            copy = pltpu.make_async_copy(
                out_ref.at[at], out_hbm.at[at], out_sem.at[n * pieces + m]
            )
            copy.start()
            sent.append(copy)
    for copy in sent:
        copy.wait()


def demig_kernel(bands, per, msg_ref, rows_hbm, out_hbm, rows_ref, out_ref, sem, out_sem):
    depth, width, long = rows_ref.shape
    block_len = long // bands
    pieces = depth // per

    def rows_copy(m):
        at = pl.ds(m * per, per)
        return pltpu.make_async_copy(rows_hbm.at[at], rows_ref.at[at], sem.at[m])

    def out_copy(start, count, slot):
        at = pl.ds(start, count)
        if len(out_ref.shape) == 4:
            at = (slice(None), at)
        return pltpu.make_async_copy(out_ref.at[at], out_hbm.at[at], out_sem.at[slot])

    for m in range(pieces):
        rows_copy(m).start()
    amp = msg_ref[:, :width]
    marks = msg_ref[:, width:].astype(F32)
    for m in range(pieces):
        rows_copy(m).wait()
        for z in range(m * per, (m + 1) * per):
            band = jnp.broadcast_to(marks[:, z : z + 1], amp.shape).astype(BF)
            rows = jnp.concatenate(
                [rows_ref[z, :, b * block_len : (b + 1) * block_len] for b in range(bands)], axis=0
            )
            put(out_ref, z, dot(by_band(band, amp, bands), rows).astype(BF))
        if m == pieces - 2:
            early = out_copy(0, (m + 1) * per, 0)
            early.start()
    late = out_copy((pieces - 1) * per, per, 1)
    late.start()
    early.wait()
    late.wait()


def residual_kernel(
    place_ref, take_ref, pick_ref, drop_ref, obs_ref, recv_ref, res_ref, send_ref, pair_ref
):
    depth = pair_ref.shape[0]
    traces, blocks, block_len = obs_ref.shape
    group = 256 // blocks
    halves = traces // group
    tiles = pick_ref.shape[0] // halves
    take = take_ref[...]
    for z in range(0, depth, 2):
        two = dot(take, jnp.concatenate([get(recv_ref, z), get(recv_ref, z + 1)], axis=1)).astype(BF)
        pair_ref[z] = two[:, :block_len]
        pair_ref[z + 1] = two[:, block_len:]
    for h in range(halves):
        total = -obs_ref[h * group : (h + 1) * group].astype(F32).reshape(group * blocks, block_len)
        for k in range(tiles):
            at = slice(k * traces + h * group, k * traces + (h + 1) * group)
            part = pair_ref[:, at, :].reshape(depth * group, block_len)
            total = total + dot(drop_ref[k * halves + h], part)
        res_ref[h * group : (h + 1) * group] = total.reshape(group, blocks, block_len)
        low = total.astype(BF)
        for k in range(tiles):
            at = slice(k * traces + h * group, k * traces + (h + 1) * group)
            got = dot(pick_ref[k * halves + h], low).astype(BF)
            pair_ref[:, at, :] = got.reshape(depth, group, block_len)
    place = place_ref[...]
    for z in range(0, depth, 2):
        two = dot(place, jnp.concatenate([pair_ref[z], pair_ref[z + 1]], axis=1)).astype(BF)
        put(send_ref, z, two[:, :block_len])
        put(send_ref, z + 1, two[:, block_len:])


def image_kernel(
    bands, per, msg_ref, amp_ref, blk_ref, tab_ref, out_hbm, stack_ref, out_ref, sem
):
    depth, width, cells = out_ref.shape
    marks = msg_ref[:, width:].astype(F32)
    sent = []
    for m in range(depth // per):
        for z in range(m * per, (m + 1) * per):
            picked = get(blk_ref, z)
            band = jnp.broadcast_to(marks[:, z : z + 1], picked.shape).astype(BF)
            masked = by_band(band, picked, bands)
            stack_ref[z * width : (z + 1) * width, :] = dot(amp_ref[...], masked).astype(BF)
        stack = stack_ref[m * per * width : (m + 1) * per * width, :]
        out_ref[m * per : (m + 1) * per] = dot(stack, tab_ref[...]).reshape(per, width, cells)
        at = pl.ds(m * per, per)
        copy = pltpu.make_async_copy(out_ref.at[at], out_hbm.at[at], sem.at[m])
        copy.start()
        sent.append(copy)
    for copy in sent:
        copy.wait()


def shards(model_image, tables, observed, aperture, traveltime, band_index, amplitude):
    devices = lax.axis_size("gx") * lax.axis_size("gy")
    depth, width_x, width_y = model_image.shape
    bands, block_len, _ = tables.shape
    traces, tile_count = aperture.shape
    blocks = observed.shape[1]
    capacity = max(2, 2 * traces * tile_count // devices)
    slots = devices * capacity
    pairs = traces * tile_count
    long = bands * block_len
    aligned = capacity % 8 == 0
    groups = pairs * blocks // 256
    tables_flat = tables.reshape(long, width_y)

    def cost(flops, moved):
        return pl.CostEstimate(flops=flops, bytes_accessed=moved, transcendentals=0)

    def shape_of(count):
        if aligned:
            return (devices, count, capacity, block_len)
        return (count, slots, block_len)

    def exchange(x):
        if not aligned:
            x = x.reshape(-1, devices, capacity, block_len).transpose(1, 0, 2, 3)
        x = lax.all_to_all(x, ("gx", "gy"), split_axis=0, concat_axis=0, tiled=True)
        if not aligned:
            x = x.transpose(1, 0, 2, 3).reshape(-1, slots, block_len)
        return x

    message, place = pl.pallas_call(
        functools.partial(prep_kernel, devices, capacity),
        out_shape=(
            jax.ShapeDtypeStruct((slots, 2 * width_x), BF),
            jax.ShapeDtypeStruct((slots, pairs), BF),
        ),
        in_specs=[VMEM] * 3,
        out_specs=(VMEM, VMEM),
        name="prep",
    )(aperture.T, band_index.transpose(1, 2, 0), amplitude)
    got = lax.all_to_all(message, ("gx", "gy"), split_axis=0, concat_axis=0, tiled=True)

    per, cols = depth // 2, long // 2
    rows = pl.pallas_call(
        functools.partial(rows_kernel, per, cols),
        out_shape=jax.ShapeDtypeStruct((depth, width_x, long), BF),
        in_specs=[ANY, ANY],
        out_specs=ANY,
        scratch_shapes=[
            pltpu.VMEM((depth, width_x, width_y), BF),
            pltpu.VMEM((long, width_y), BF),
            pltpu.VMEM((long // cols, width_y, cols), BF),
            pltpu.VMEM((depth, width_x, long), BF),
            pltpu.SemaphoreType.DMA((depth // per,)),
            pltpu.SemaphoreType.DMA((long // cols,)),
            pltpu.SemaphoreType.DMA((depth // per * (long // cols),)),
        ],
        cost_estimate=cost(2 * depth * width_x * width_y * long, 4 * depth * width_x * width_y),
        name="rows",
    )(model_image, tables_flat)
    rows = pltpu.with_memory_space_constraint(rows, pltpu.HBM)
    per = 4
    partials = pl.pallas_call(
        functools.partial(demig_kernel, bands, per),
        out_shape=jax.ShapeDtypeStruct(shape_of(depth), BF),
        in_specs=[VMEM, ANY],
        out_specs=ANY,
        scratch_shapes=[
            pltpu.VMEM((depth, width_x, long), BF),
            pltpu.VMEM(shape_of(depth), BF),
            pltpu.SemaphoreType.DMA((depth // per,)),
            pltpu.SemaphoreType.DMA((2,)),
        ],
        compiler_params=GRANT,
        cost_estimate=cost(2 * depth * slots * width_x * long, 2 * depth * width_x * long),
        name="demig",
    )(got, rows)
    returned = exchange(partials)
    take, pick, drop, turned = pl.pallas_call(
        functools.partial(codes_kernel, blocks),
        out_shape=(
            jax.ShapeDtypeStruct((pairs, slots), BF),
            jax.ShapeDtypeStruct((groups, 256, 256), BF),
            jax.ShapeDtypeStruct((groups, 256, 256), BF),
            jax.ShapeDtypeStruct((width_x, slots), BF),
        ),
        in_specs=[VMEM] * 3,
        out_specs=(VMEM,) * 4,
        compiler_params=GRANT,
        cost_estimate=cost(groups * 256 * 256 * 256, groups * 256 * 256 * 4),
        name="codes",
    )(got, place, traveltime.transpose(1, 2, 0))
    residual, outgoing = pl.pallas_call(
        residual_kernel,
        out_shape=(
            jax.ShapeDtypeStruct((traces, blocks, block_len), F32),
            jax.ShapeDtypeStruct(shape_of(depth), BF),
        ),
        in_specs=[VMEM] * 6,
        out_specs=(VMEM, VMEM),
        scratch_shapes=[pltpu.VMEM((depth, pairs, block_len), BF)],
        compiler_params=GRANT,
        cost_estimate=cost(4 * depth * slots * pairs * block_len, 4 * depth * slots * block_len),
        name="resid",
    )(place, take, pick, drop, observed, returned)
    incoming = exchange(outgoing)
    per = 2
    gradient = pl.pallas_call(
        functools.partial(image_kernel, bands, per),
        out_shape=jax.ShapeDtypeStruct((depth, width_x, width_y), F32),
        in_specs=[VMEM] * 4,
        out_specs=ANY,
        scratch_shapes=[
            pltpu.VMEM((depth * width_x, long), BF),
            pltpu.VMEM((depth, width_x, width_y), F32),
            pltpu.SemaphoreType.DMA((depth // per,)),
        ],
        compiler_params=pltpu.CompilerParams(vmem_limit_bytes=32 * 1024 * 1024),
        cost_estimate=cost(
            2 * depth * width_x * long * (width_y + slots), 4 * depth * width_x * width_y
        ),
        name="image",
    )(got, turned, incoming, tables_flat)
    return residual, gradient


def solution(mesh):
    both = ("gx", "gy")
    placed = (
        P(None, "gx", "gy"),
        P(),
        P(both, None, None),
        P(both, None),
        P(both, None, None),
        P(both, None, None),
        P(both, None, None),
    )
    return jax.shard_map(
        shards,
        mesh=mesh,
        in_specs=placed,
        out_specs=(P(both, None, None), P(None, "gx", "gy")),
        check_vma=False,
    )
```

```python
import functools

import jax
import jax.numpy as jnp
from jax import lax
from jax.experimental import pallas as pl
from jax.experimental.pallas import tpu as pltpu
from jax.sharding import PartitionSpec as P

BF = jnp.bfloat16
F32 = jnp.float32
GRANT = pltpu.CompilerParams(vmem_limit_bytes=20 * 1024 * 1024)
ANY = pl.BlockSpec(memory_space=pl.ANY)
VMEM = pl.BlockSpec(memory_space=pltpu.VMEM)


def dot(a, b, dims=((1,), (0,))):
    return lax.dot_general(a, b, (dims, ((), ())), preferred_element_type=F32)


def iota(shape, axis):
    return lax.broadcasted_iota(jnp.int32, shape, axis)


def prep_kernel(devices, capacity, ap_ref, bi_ref, am_ref, msg_ref, place_ref):
    tiles, traces = ap_ref.shape
    slots = devices * capacity
    width = am_ref.shape[2]
    depth = bi_ref.shape[1]
    before = (iota((traces, traces), 0) < iota((traces, traces), 1)).astype(BF)
    base = jnp.zeros((devices, 1), F32)
    amp = jnp.zeros((slots, width), F32)
    marks = jnp.zeros((slots, width), F32)
    for k in range(tiles):
        dest = ap_ref[k : k + 1, :]
        hit = iota((devices, traces), 0) == dest
        hits = hit.astype(F32)
        rank = jnp.sum(hits * (base + dot(hits.astype(BF), before)), axis=0, keepdims=True)
        base = base + jnp.sum(hits, axis=1, keepdims=True)
        pos = dest * capacity + rank.astype(jnp.int32)
        place = (iota((slots, traces), 0) == pos).astype(F32).astype(BF)
        place_ref[:, k * traces : (k + 1) * traces] = place
        amp = amp + dot(place, am_ref[:, k, :])
        levels = jnp.concatenate(
            [bi_ref[k].astype(F32), jnp.zeros((width - depth, traces), F32)], axis=0
        ).astype(BF)
        marks = marks + dot(place, levels, ((1,), (1,)))
    msg_ref[:, :width] = amp.astype(BF)
    msg_ref[:, width:] = marks.astype(BF)


def codes_kernel(blocks, msg_ref, place_ref, tt_ref, take_ref, pick_ref, drop_ref, amp_ref):
    tiles, depth, traces = tt_ref.shape
    group = 256 // blocks
    width = amp_ref.shape[0]
    amp_ref[...] = msg_ref[:, :width].astype(F32).T.astype(BF)
    take_ref[...] = place_ref[...].astype(F32).T.astype(BF)
    size = depth * group
    lanes = 128
    at = iota((size, lanes), 1).astype(F32).astype(BF)
    row = iota((size, 1), 0)
    level = (row // group == iota((size, depth), 1)).astype(F32).astype(BF)
    for k in range(tiles):
        times = dot(level, tt_ref[k].astype(F32).astype(BF))
        for h in range(traces // group):
            own = iota((size, traces), 1) == row % group + h * group
            code = jnp.where(own, times, 0.0).astype(BF)
            code = dot(code, jnp.ones((traces, lanes), F32).astype(BF))
            code = (code + (row % group * blocks).astype(F32)).astype(BF)
            one, zero = jnp.ones_like(code), jnp.zeros_like(code)
            pick = jnp.concatenate(
                [jnp.where(code == at + BF(i), one, zero) for i in range(0, group * blocks, lanes)],
                axis=1,
            )
            pick_ref[k * (traces // group) + h] = pick
            drop_ref[k * (traces // group) + h] = pick.astype(F32).T.astype(BF)


def by_band(band, values, bands):
    zero = jnp.zeros_like(values)
    return jnp.concatenate([jnp.where(band == BF(b), values, zero) for b in range(bands)], axis=1)


def put(ref, z, value):
    if len(ref.shape) == 4:
        ref[:, z] = value.reshape(ref.shape[0], ref.shape[2], ref.shape[3])
    else:
        ref[z] = value


def get(ref, z):
    if len(ref.shape) == 4:
        return ref[:, z].reshape(ref.shape[0] * ref.shape[2], ref.shape[3])
    return ref[z]


def rows_kernel(
    per,
    cols,
    image_hbm,
    tab_hbm,
    out_hbm,
    image_ref,
    tab_ref,
    turn_ref,
    out_ref,
    image_sem,
    tab_sem,
    out_sem,
):
    depth, width, cells = image_ref.shape
    pieces, strips = depth // per, tab_ref.shape[0] // cols

    def image_copy(m):
        at = pl.ds(m * per, per)
        return pltpu.make_async_copy(image_hbm.at[at], image_ref.at[at], image_sem.at[m])

    def tab_copy(n):
        at = pl.ds(n * cols, cols)
        return pltpu.make_async_copy(tab_hbm.at[at], tab_ref.at[at], tab_sem.at[n])

    tab_copy(0).start()
    for m in range(pieces):
        image_copy(m).start()
    for n in range(1, strips):
        tab_copy(n).start()
    sent = []
    tab_copy(0).wait()
    turn_ref[0] = tab_ref[:cols, :].T
    for n in range(strips):
        for m in range(pieces):
            if n == 0:
                image_copy(m).wait()
            if m == pieces - 1 and n + 1 < strips:
                tab_copy(n + 1).wait()
                turn_ref[n + 1] = tab_ref[(n + 1) * cols : (n + 2) * cols, :].T
            last = n == strips - 1 and m == pieces - 1
            part = per // 2 if last else per
            for start in range(m * per, (m + 1) * per, part):
                levels = image_ref[start : start + part].reshape(part * width, cells)
                rows = dot(levels, turn_ref[n]).astype(BF)
                out_ref[start : start + part, :, n * cols : (n + 1) * cols] = rows.reshape(
                    part, width, cols
                )
                at = (pl.ds(start, part), slice(None), pl.ds(n * cols, cols))
                copy = pltpu.make_async_copy(out_ref.at[at], out_hbm.at[at], out_sem.at[len(sent)])
                copy.start()
                sent.append(copy)
    for copy in sent:
        copy.wait()


def demig_kernel(bands, per, msg_ref, rows_hbm, out_ref, rows_ref, sem):
    depth, width, long = rows_ref.shape
    block_len = long // bands
    pieces = depth // per

    def rows_copy(m):
        at = pl.ds(m * per, per)
        return pltpu.make_async_copy(rows_hbm.at[at], rows_ref.at[at], sem.at[m])

    for m in range(pieces):
        rows_copy(m).start()
    amp = msg_ref[:, :width]
    marks = msg_ref[:, width:].astype(F32)
    for m in range(pieces):
        rows_copy(m).wait()
        for z in range(m * per, (m + 1) * per):
            band = jnp.broadcast_to(marks[:, z : z + 1], amp.shape).astype(BF)
            rows = jnp.concatenate(
                [rows_ref[z, :, b * block_len : (b + 1) * block_len] for b in range(bands)], axis=0
            )
            put(out_ref, z, dot(by_band(band, amp, bands), rows).astype(BF))


def residual_kernel(
    place_ref, take_ref, pick_ref, drop_ref, obs_ref, recv_ref, res_ref, send_ref, pair_ref
):
    depth = pair_ref.shape[0]
    traces, blocks, block_len = obs_ref.shape
    group = 256 // blocks
    halves = traces // group
    tiles = pick_ref.shape[0] // halves
    take = take_ref[...]
    for z in range(0, depth, 2):
        two = dot(take, jnp.concatenate([get(recv_ref, z), get(recv_ref, z + 1)], axis=1)).astype(BF)
        pair_ref[z] = two[:, :block_len]
        pair_ref[z + 1] = two[:, block_len:]
    for h in range(halves):
        total = -obs_ref[h * group : (h + 1) * group].astype(F32).reshape(group * blocks, block_len)
        for k in range(tiles):
            at = slice(k * traces + h * group, k * traces + (h + 1) * group)
            part = pair_ref[:, at, :].reshape(depth * group, block_len)
            total = total + dot(drop_ref[k * halves + h], part)
        res_ref[h * group : (h + 1) * group] = total.reshape(group, blocks, block_len)
        low = total.astype(BF)
        for k in range(tiles):
            at = slice(k * traces + h * group, k * traces + (h + 1) * group)
            got = dot(pick_ref[k * halves + h], low).astype(BF)
            pair_ref[:, at, :] = got.reshape(depth, group, block_len)
    place = place_ref[...]
    for z in range(0, depth, 2):
        two = dot(place, jnp.concatenate([pair_ref[z], pair_ref[z + 1]], axis=1)).astype(BF)
        put(send_ref, z, two[:, :block_len])
        put(send_ref, z + 1, two[:, block_len:])


def image_kernel(
    bands, per, msg_ref, amp_ref, blk_ref, tab_ref, out_hbm, stack_ref, out_ref, sem
):
    depth, width, cells = out_ref.shape
    marks = msg_ref[:, width:].astype(F32)
    sent = []
    for m in range(depth // per):
        for z in range(m * per, (m + 1) * per):
            picked = get(blk_ref, z)
            band = jnp.broadcast_to(marks[:, z : z + 1], picked.shape).astype(BF)
            masked = by_band(band, picked, bands)
            stack_ref[z * width : (z + 1) * width, :] = dot(amp_ref[...], masked).astype(BF)
        stack = stack_ref[m * per * width : (m + 1) * per * width, :]
        out_ref[m * per : (m + 1) * per] = dot(stack, tab_ref[...]).reshape(per, width, cells)
        at = pl.ds(m * per, per)
        copy = pltpu.make_async_copy(out_ref.at[at], out_hbm.at[at], sem.at[m])
        copy.start()
        sent.append(copy)
    for copy in sent:
        copy.wait()


def shards(model_image, tables, observed, aperture, traveltime, band_index, amplitude):
    devices = lax.axis_size("gx") * lax.axis_size("gy")
    depth, width_x, width_y = model_image.shape
    bands, block_len, _ = tables.shape
    traces, tile_count = aperture.shape
    blocks = observed.shape[1]
    capacity = max(2, 2 * traces * tile_count // devices)
    slots = devices * capacity
    pairs = traces * tile_count
    long = bands * block_len
    aligned = capacity % 8 == 0
    groups = pairs * blocks // 256
    tables_flat = tables.reshape(long, width_y)

    def cost(flops, moved):
        return pl.CostEstimate(flops=flops, bytes_accessed=moved, transcendentals=0)

    def shape_of(count):
        if aligned:
            return (devices, count, capacity, block_len)
        return (count, slots, block_len)

    def exchange(x):
        if not aligned:
            x = x.reshape(-1, devices, capacity, block_len).transpose(1, 0, 2, 3)
        x = lax.all_to_all(x, ("gx", "gy"), split_axis=0, concat_axis=0, tiled=True)
        if not aligned:
            x = x.transpose(1, 0, 2, 3).reshape(-1, slots, block_len)
        return x

    message, place = pl.pallas_call(
        functools.partial(prep_kernel, devices, capacity),
        out_shape=(
            jax.ShapeDtypeStruct((slots, 2 * width_x), BF),
            jax.ShapeDtypeStruct((slots, pairs), BF),
        ),
        in_specs=[VMEM] * 3,
        out_specs=(VMEM, VMEM),
        name="prep",
    )(aperture.T, band_index.transpose(1, 2, 0), amplitude)
    got = lax.all_to_all(message, ("gx", "gy"), split_axis=0, concat_axis=0, tiled=True)

    per, cols = depth // 2, long // 2
    rows = pl.pallas_call(
        functools.partial(rows_kernel, per, cols),
        out_shape=jax.ShapeDtypeStruct((depth, width_x, long), BF),
        in_specs=[ANY, ANY],
        out_specs=ANY,
        scratch_shapes=[
            pltpu.VMEM((depth, width_x, width_y), BF),
            pltpu.VMEM((long, width_y), BF),
            pltpu.VMEM((long // cols, width_y, cols), BF),
            pltpu.VMEM((depth, width_x, long), BF),
            pltpu.SemaphoreType.DMA((depth // per,)),
            pltpu.SemaphoreType.DMA((long // cols,)),
            pltpu.SemaphoreType.DMA((depth // per * (long // cols) + 1,)),
        ],
        cost_estimate=cost(2 * depth * width_x * width_y * long, 4 * depth * width_x * width_y),
        name="rows",
    )(model_image, tables_flat)
    rows = pltpu.with_memory_space_constraint(rows, pltpu.HBM)
    per = 4
    partials = pl.pallas_call(
        functools.partial(demig_kernel, bands, per),
        out_shape=jax.ShapeDtypeStruct(shape_of(depth), BF),
        in_specs=[VMEM, ANY],
        out_specs=VMEM,
        scratch_shapes=[
            pltpu.VMEM((depth, width_x, long), BF),
            pltpu.SemaphoreType.DMA((depth // per,)),
        ],
        compiler_params=GRANT,
        cost_estimate=cost(2 * depth * slots * width_x * long, 2 * depth * width_x * long),
        name="demig",
    )(got, rows)
    returned = exchange(partials)
    take, pick, drop, turned = pl.pallas_call(
        functools.partial(codes_kernel, blocks),
        out_shape=(
            jax.ShapeDtypeStruct((pairs, slots), BF),
            jax.ShapeDtypeStruct((groups, 256, 256), BF),
            jax.ShapeDtypeStruct((groups, 256, 256), BF),
            jax.ShapeDtypeStruct((width_x, slots), BF),
        ),
        in_specs=[VMEM] * 3,
        out_specs=(VMEM,) * 4,
        compiler_params=GRANT,
        cost_estimate=cost(groups * 256 * 256 * 256, groups * 256 * 256 * 4),
        name="codes",
    )(got, place, traveltime.transpose(1, 2, 0))
    residual, outgoing = pl.pallas_call(
        residual_kernel,
        out_shape=(
            jax.ShapeDtypeStruct((traces, blocks, block_len), F32),
            jax.ShapeDtypeStruct(shape_of(depth), BF),
        ),
        in_specs=[VMEM] * 6,
        out_specs=(VMEM, VMEM),
        scratch_shapes=[pltpu.VMEM((depth, pairs, block_len), BF)],
        compiler_params=GRANT,
        cost_estimate=cost(4 * depth * slots * pairs * block_len, 4 * depth * slots * block_len),
        name="resid",
    )(place, take, pick, drop, observed, returned)
    incoming = exchange(outgoing)
    per = 2
    gradient = pl.pallas_call(
        functools.partial(image_kernel, bands, per),
        out_shape=jax.ShapeDtypeStruct((depth, width_x, width_y), F32),
        in_specs=[VMEM] * 4,
        out_specs=ANY,
        scratch_shapes=[
            pltpu.VMEM((depth * width_x, long), BF),
            pltpu.VMEM((depth, width_x, width_y), F32),
            pltpu.SemaphoreType.DMA((depth // per,)),
        ],
        compiler_params=pltpu.CompilerParams(vmem_limit_bytes=32 * 1024 * 1024),
        cost_estimate=cost(
            2 * depth * width_x * long * (width_y + slots), 4 * depth * width_x * width_y
        ),
        name="image",
    )(got, turned, incoming, tables_flat)
    return residual, gradient


def solution(mesh):
    both = ("gx", "gy")
    placed = (
        P(None, "gx", "gy"),
        P(),
        P(both, None, None),
        P(both, None),
        P(both, None, None),
        P(both, None, None),
        P(both, None, None),
    )
    return jax.shard_map(
        shards,
        mesh=mesh,
        in_specs=placed,
        out_specs=(P(both, None, None), P(None, "gx", "gy")),
        check_vma=False,
    )
```

```python
import functools

import jax
import jax.numpy as jnp
from jax import lax
from jax.experimental import pallas as pl
from jax.experimental.pallas import tpu as pltpu
from jax.sharding import PartitionSpec as P

BF = jnp.bfloat16
F32 = jnp.float32
GRANT = pltpu.CompilerParams(vmem_limit_bytes=20 * 1024 * 1024)
ANY = pl.BlockSpec(memory_space=pl.ANY)
VMEM = pl.BlockSpec(memory_space=pltpu.VMEM)


def dot(a, b, dims=((1,), (0,))):
    return lax.dot_general(a, b, (dims, ((), ())), preferred_element_type=F32)


def iota(shape, axis):
    return lax.broadcasted_iota(jnp.int32, shape, axis)


def prep_kernel(devices, capacity, ap_ref, bi_ref, am_ref, msg_ref, place_ref):
    tiles, traces = ap_ref.shape
    slots = devices * capacity
    width = am_ref.shape[2]
    depth = bi_ref.shape[1]
    before = (iota((traces, traces), 0) < iota((traces, traces), 1)).astype(BF)
    base = jnp.zeros((devices, 1), F32)
    amp = jnp.zeros((slots, width), F32)
    marks = jnp.zeros((slots, width), F32)
    for k in range(tiles):
        dest = ap_ref[k : k + 1, :]
        hit = iota((devices, traces), 0) == dest
        hits = hit.astype(F32)
        rank = jnp.sum(hits * (base + dot(hits.astype(BF), before)), axis=0, keepdims=True)
        base = base + jnp.sum(hits, axis=1, keepdims=True)
        pos = dest * capacity + rank.astype(jnp.int32)
        place = (iota((slots, traces), 0) == pos).astype(F32).astype(BF)
        place_ref[:, k * traces : (k + 1) * traces] = place
        amp = amp + dot(place, am_ref[:, k, :])
        levels = jnp.concatenate(
            [bi_ref[k].astype(F32), jnp.zeros((width - depth, traces), F32)], axis=0
        ).astype(BF)
        marks = marks + dot(place, levels, ((1,), (1,)))
    msg_ref[:, :width] = amp.astype(BF)
    msg_ref[:, width:] = marks.astype(BF)


def codes_kernel(blocks, msg_ref, place_ref, tt_ref, take_ref, pick_ref, drop_ref, amp_ref):
    tiles, depth, traces = tt_ref.shape
    group = 256 // blocks
    width = amp_ref.shape[0]
    amp_ref[...] = msg_ref[:, :width].astype(F32).T.astype(BF)
    take_ref[...] = place_ref[...].astype(F32).T.astype(BF)
    size = depth * group
    lanes = 128
    at = iota((size, lanes), 1).astype(F32).astype(BF)
    row = iota((size, 1), 0)
    level = (row // group == iota((size, depth), 1)).astype(F32).astype(BF)
    for k in range(tiles):
        times = dot(level, tt_ref[k].astype(F32).astype(BF))
        for h in range(traces // group):
            own = iota((size, traces), 1) == row % group + h * group
            code = jnp.where(own, times, 0.0).astype(BF)
            code = dot(code, jnp.ones((traces, lanes), F32).astype(BF))
            code = (code + (row % group * blocks).astype(F32)).astype(BF)
            one, zero = jnp.ones_like(code), jnp.zeros_like(code)
            pick = jnp.concatenate(
                [jnp.where(code == at + BF(i), one, zero) for i in range(0, group * blocks, lanes)],
                axis=1,
            )
            pick_ref[k * (traces // group) + h] = pick
            drop_ref[k * (traces // group) + h] = pick.astype(F32).T.astype(BF)


def by_band(band, values, bands):
    zero = jnp.zeros_like(values)
    return jnp.concatenate([jnp.where(band == BF(b), values, zero) for b in range(bands)], axis=1)


def put(ref, z, value):
    if len(ref.shape) == 4:
        ref[:, z] = value.reshape(ref.shape[0], ref.shape[2], ref.shape[3])
    else:
        ref[z] = value


def get(ref, z):
    if len(ref.shape) == 4:
        return ref[:, z].reshape(ref.shape[0] * ref.shape[2], ref.shape[3])
    return ref[z]


def rows_kernel(
    per,
    cols,
    image_hbm,
    tab_hbm,
    out_hbm,
    image_ref,
    tab_ref,
    turn_ref,
    out_ref,
    image_sem,
    tab_sem,
    out_sem,
):
    depth, width, cells = image_ref.shape
    pieces, strips = depth // per, tab_ref.shape[0] // cols

    def image_copy(m):
        at = pl.ds(m * per, per)
        return pltpu.make_async_copy(image_hbm.at[at], image_ref.at[at], image_sem.at[m])

    def tab_copy(n):
        at = pl.ds(n * cols, cols)
        return pltpu.make_async_copy(tab_hbm.at[at], tab_ref.at[at], tab_sem.at[n])

    tab_copy(0).start()
    for m in range(pieces):
        image_copy(m).start()
    for n in range(1, strips):
        tab_copy(n).start()
    sent = []
    tab_copy(0).wait()
    turn_ref[0] = tab_ref[:cols, :].T
    for n in range(strips):
        for m in range(pieces):
            if n == 0:
                image_copy(m).wait()
            if m == pieces - 1 and n + 1 < strips:
                tab_copy(n + 1).wait()
                turn_ref[n + 1] = tab_ref[(n + 1) * cols : (n + 2) * cols, :].T
            levels = image_ref[m * per : (m + 1) * per].reshape(per * width, cells)
            rows = dot(levels, turn_ref[n]).astype(BF)
            out_ref[m * per : (m + 1) * per, :, n * cols : (n + 1) * cols] = rows.reshape(
                per, width, cols
            )
            at = (pl.ds(m * per, per), slice(None), pl.ds(n * cols, cols))
            copy = pltpu.make_async_copy(
                out_ref.at[at], out_hbm.at[at], out_sem.at[n * pieces + m]
            )
            copy.start()
            sent.append(copy)
    for copy in sent:
        copy.wait()


def demig_kernel(bands, per, msg_ref, rows_hbm, out_ref, rows_ref, sem):
    depth, width, long = rows_ref.shape
    block_len = long // bands
    pieces = depth // per

    def rows_copy(m):
        at = pl.ds(m * per, per)
        return pltpu.make_async_copy(rows_hbm.at[at], rows_ref.at[at], sem.at[m])

    for m in range(pieces):
        rows_copy(m).start()
    amp = msg_ref[:, :width]
    marks = msg_ref[:, width:].astype(F32)
    for m in range(pieces):
        rows_copy(m).wait()
        for z in range(m * per, (m + 1) * per):
            band = jnp.broadcast_to(marks[:, z : z + 1], amp.shape).astype(BF)
            rows = jnp.concatenate(
                [rows_ref[z, :, b * block_len : (b + 1) * block_len] for b in range(bands)], axis=0
            )
            put(out_ref, z, dot(by_band(band, amp, bands), rows).astype(BF))


def residual_kernel(
    place_ref, take_ref, pick_ref, drop_ref, obs_ref, recv_ref, res_ref, send_ref, pair_ref
):
    depth = pair_ref.shape[0]
    traces, blocks, block_len = obs_ref.shape
    group = 256 // blocks
    halves = traces // group
    tiles = pick_ref.shape[0] // halves
    take = take_ref[...]
    for z in range(0, depth, 2):
        two = dot(take, jnp.concatenate([get(recv_ref, z), get(recv_ref, z + 1)], axis=1)).astype(BF)
        pair_ref[z] = two[:, :block_len]
        pair_ref[z + 1] = two[:, block_len:]
    for h in range(halves):
        total = -obs_ref[h * group : (h + 1) * group].astype(F32).reshape(group * blocks, block_len)
        for k in range(tiles):
            at = slice(k * traces + h * group, k * traces + (h + 1) * group)
            part = pair_ref[:, at, :].reshape(depth * group, block_len)
            total = total + dot(drop_ref[k * halves + h], part)
        res_ref[h * group : (h + 1) * group] = total.reshape(group, blocks, block_len)
        low = total.astype(BF)
        for k in range(tiles):
            at = slice(k * traces + h * group, k * traces + (h + 1) * group)
            got = dot(pick_ref[k * halves + h], low).astype(BF)
            pair_ref[:, at, :] = got.reshape(depth, group, block_len)
    place = place_ref[...]
    for z in range(0, depth, 2):
        two = dot(place, jnp.concatenate([pair_ref[z], pair_ref[z + 1]], axis=1)).astype(BF)
        put(send_ref, z, two[:, :block_len])
        put(send_ref, z + 1, two[:, block_len:])


def image_kernel(
    bands, per, msg_ref, amp_ref, blk_ref, tab_ref, out_hbm, stack_ref, out_ref, sem
):
    depth, width, cells = out_ref.shape
    marks = msg_ref[:, width:].astype(F32)
    sent = []
    for m in range(depth // per):
        for z in range(m * per, (m + 1) * per):
            picked = get(blk_ref, z)
            band = jnp.broadcast_to(marks[:, z : z + 1], picked.shape).astype(BF)
            masked = by_band(band, picked, bands)
            stack_ref[z * width : (z + 1) * width, :] = dot(amp_ref[...], masked).astype(BF)
        stack = stack_ref[m * per * width : (m + 1) * per * width, :]
        out_ref[m * per : (m + 1) * per] = dot(stack, tab_ref[...]).reshape(per, width, cells)
        at = pl.ds(m * per, per)
        copy = pltpu.make_async_copy(out_ref.at[at], out_hbm.at[at], sem.at[m])
        copy.start()
        sent.append(copy)
    for copy in sent:
        copy.wait()


def shards(model_image, tables, observed, aperture, traveltime, band_index, amplitude):
    devices = lax.axis_size("gx") * lax.axis_size("gy")
    depth, width_x, width_y = model_image.shape
    bands, block_len, _ = tables.shape
    traces, tile_count = aperture.shape
    blocks = observed.shape[1]
    capacity = max(2, 2 * traces * tile_count // devices)
    slots = devices * capacity
    pairs = traces * tile_count
    long = bands * block_len
    aligned = capacity % 8 == 0
    groups = pairs * blocks // 256
    tables_flat = tables.reshape(long, width_y)

    def cost(flops, moved):
        return pl.CostEstimate(flops=flops, bytes_accessed=moved, transcendentals=0)

    def shape_of(count):
        if aligned:
            return (devices, count, capacity, block_len)
        return (count, slots, block_len)

    def exchange(x):
        if not aligned:
            x = x.reshape(-1, devices, capacity, block_len).transpose(1, 0, 2, 3)
        x = lax.all_to_all(x, ("gx", "gy"), split_axis=0, concat_axis=0, tiled=True)
        if not aligned:
            x = x.transpose(1, 0, 2, 3).reshape(-1, slots, block_len)
        return x

    message, place = pl.pallas_call(
        functools.partial(prep_kernel, devices, capacity),
        out_shape=(
            jax.ShapeDtypeStruct((slots, 2 * width_x), BF),
            jax.ShapeDtypeStruct((slots, pairs), BF),
        ),
        in_specs=[VMEM] * 3,
        out_specs=(VMEM, VMEM),
        name="prep",
    )(aperture.T, band_index.transpose(1, 2, 0), amplitude)
    got = lax.all_to_all(message, ("gx", "gy"), split_axis=0, concat_axis=0, tiled=True)

    per, cols = depth // 2, long // 2
    rows = pl.pallas_call(
        functools.partial(rows_kernel, per, cols),
        out_shape=jax.ShapeDtypeStruct((depth, width_x, long), BF),
        in_specs=[ANY, ANY],
        out_specs=ANY,
        scratch_shapes=[
            pltpu.VMEM((depth, width_x, width_y), BF),
            pltpu.VMEM((long, width_y), BF),
            pltpu.VMEM((long // cols, width_y, cols), BF),
            pltpu.VMEM((depth, width_x, long), BF),
            pltpu.SemaphoreType.DMA((depth // per,)),
            pltpu.SemaphoreType.DMA((long // cols,)),
            pltpu.SemaphoreType.DMA((depth // per * (long // cols),)),
        ],
        cost_estimate=cost(2 * depth * width_x * width_y * long, 4 * depth * width_x * width_y),
        name="rows",
    )(model_image, tables_flat)
    rows = pltpu.with_memory_space_constraint(rows, pltpu.HBM)
    per = depth // 2
    partials = pl.pallas_call(
        functools.partial(demig_kernel, bands, per),
        out_shape=jax.ShapeDtypeStruct(shape_of(depth), BF),
        in_specs=[VMEM, ANY],
        out_specs=VMEM,
        scratch_shapes=[
            pltpu.VMEM((depth, width_x, long), BF),
            pltpu.SemaphoreType.DMA((depth // per,)),
        ],
        compiler_params=GRANT,
        cost_estimate=cost(2 * depth * slots * width_x * long, 2 * depth * width_x * long),
        name="demig",
    )(got, rows)
    returned = exchange(partials)
    take, pick, drop, turned = pl.pallas_call(
        functools.partial(codes_kernel, blocks),
        out_shape=(
            jax.ShapeDtypeStruct((pairs, slots), BF),
            jax.ShapeDtypeStruct((groups, 256, 256), BF),
            jax.ShapeDtypeStruct((groups, 256, 256), BF),
            jax.ShapeDtypeStruct((width_x, slots), BF),
        ),
        in_specs=[VMEM] * 3,
        out_specs=(VMEM,) * 4,
        compiler_params=GRANT,
        cost_estimate=cost(groups * 256 * 256 * 256, groups * 256 * 256 * 4),
        name="codes",
    )(got, place, traveltime.transpose(1, 2, 0))
    residual, outgoing = pl.pallas_call(
        residual_kernel,
        out_shape=(
            jax.ShapeDtypeStruct((traces, blocks, block_len), F32),
            jax.ShapeDtypeStruct(shape_of(depth), BF),
        ),
        in_specs=[VMEM] * 6,
        out_specs=(VMEM, VMEM),
        scratch_shapes=[pltpu.VMEM((depth, pairs, block_len), BF)],
        compiler_params=GRANT,
        cost_estimate=cost(4 * depth * slots * pairs * block_len, 4 * depth * slots * block_len),
        name="resid",
    )(place, take, pick, drop, observed, returned)
    incoming = exchange(outgoing)
    per = 2
    gradient = pl.pallas_call(
        functools.partial(image_kernel, bands, per),
        out_shape=jax.ShapeDtypeStruct((depth, width_x, width_y), F32),
        in_specs=[VMEM] * 4,
        out_specs=ANY,
        scratch_shapes=[
            pltpu.VMEM((depth * width_x, long), BF),
            pltpu.VMEM((depth, width_x, width_y), F32),
            pltpu.SemaphoreType.DMA((depth // per,)),
        ],
        compiler_params=pltpu.CompilerParams(vmem_limit_bytes=32 * 1024 * 1024),
        cost_estimate=cost(
            2 * depth * width_x * long * (width_y + slots), 4 * depth * width_x * width_y
        ),
        name="image",
    )(got, turned, incoming, tables_flat)
    return residual, gradient


def solution(mesh):
    both = ("gx", "gy")
    placed = (
        P(None, "gx", "gy"),
        P(),
        P(both, None, None),
        P(both, None),
        P(both, None, None),
        P(both, None, None),
        P(both, None, None),
    )
    return jax.shard_map(
        shards,
        mesh=mesh,
        in_specs=placed,
        out_specs=(P(both, None, None), P(None, "gx", "gy")),
        check_vma=False,
    )
```
